32 devices in a mesh: heads: 8 (over z, x), ctx: 4 (over y, core).
Axes of the slice: x: 2, y: 2, z: 4, core: 2. Of those that a mesh axis runs over, the one named last changes fastest.
Arguments:
- queries: bfloat16 [4096, 4096], P(('ctx', 'heads')), may hold values from -500 to 500
- keys_in: bfloat16 [4096, 512], P(('ctx', 'heads')), may hold values from -7 to 7
- values_in: bfloat16 [4096, 512], P(('ctx', 'heads')), may hold values from -6 to 6
- cotangent: bfloat16 [4096, 4096], P(('ctx', 'heads')), may hold values from -6 to 6
- rand_blocks: int32 [32, 1], replicated, may hold values from 0 to 31, as said below
- glob_blocks: int32 [2], replicated, may hold values from 0 to 31
Outputs:
- attn_out: bfloat16 [4096, 4096], P(('ctx', 'heads'))
- grad_query: bfloat16 [4096, 4096], P(('ctx', 'heads'))
- grad_keys: bfloat16 [4096, 512], P(('ctx', 'heads'))
- grad_values: bfloat16 [4096, 512], P(('ctx', 'heads'))
The draws below stay inside these ranges and needn't reach their ends.
Inputs may be any that keep to these rules, and one draw needn't show every extreme that they name: `rand_blocks`: of the 8 entries in the rows of one segment's query blocks (rows c*8 to (c+1)*8 - 1), exactly 2 name blocks of each segment (blocks s*8 to (s+1)*8 - 1).
All inputs are finite; a program needn't handle non-finite values.
Results may differ from the reference program's by a relative error of at most 0.0075.
Values may be sent and summed in bfloat16 or wider, within the bound.
No kernel may reach another device: no remote copies, remote signals or barrier semaphores. Data moves between devices by JAX's collectives and lax.ppermute only.
A program may use at most 128 MiB of HBM per device.

```python
import math
import jax
import jax.numpy as jnp
from jax import lax

HD = 128
H = 32
KVH = 4
BLK = 128
NG = 2
NR = 1
TOKENS = 4096
QB = 8
NB = 32
CAP = 2
NK = 6
N_CTX = 4


def common_rows(key):
    drawn_keys = jnp.clip(jax.random.normal(jax.random.fold_in(key, 3), (TOKENS, KVH * HD), jnp.float32), -6.0, 6.0)
    return drawn_keys


def draw_keys_in(key, part):
    drawn_keys = common_rows(key)
    return drawn_keys.astype(jnp.bfloat16)


def draw_queries(key, part):
    drawn_queries = jnp.clip(jax.random.normal(jax.random.fold_in(key, 7), (TOKENS, H * HD), jnp.float32), -6.0, 6.0)
    return drawn_queries.astype(jnp.bfloat16)


def draw_rand_blocks(key, part):
    request_count = QB * NR
    pattern = jnp.tile(jnp.arange(N_CTX, dtype=jnp.int32), CAP)
    owner_keys = jax.random.split(jax.random.fold_in(key, 9), N_CTX)
    owners = jax.vmap(lambda one_key: jax.random.permutation(one_key, pattern))(owner_keys)
    local_ids = jax.random.randint(jax.random.fold_in(key, 13), (N_CTX, request_count), 0, QB, dtype=jnp.int32)
    return (owners * QB + local_ids).reshape(NB, NR)


def block_levels(own_key, dims, shards, smallest, high):
    def one(dim, parts):
        heights = jax.random.uniform(jax.random.fold_in(jax.random.fold_in(own_key, 6), dim), (parts,), jnp.float32, smallest / len(shards), high / len(shards))
        return jnp.repeat(jnp.exp(heights), dims[dim] // parts).reshape((-1,) + (1,) * (len(dims) - dim - 1))

    factor_of = one(*shards[0])
    for cut in shards[1:]:
        factor_of = factor_of * one(*cut)
    return factor_of


def bell_draw(own_key, dims, scale, bound, pieces=(), held_as=jnp.bfloat16):
    values = jax.random.normal(own_key, dims, jnp.float32) * scale
    if len(pieces) > 0:
        values = block_levels(own_key, dims, pieces, -0.22, 0.18) * values
    return jnp.clip(values, min=-bound, max=bound).astype(held_as)


def setup_inputs(seed: int = 0) -> dict:
    arg_keys = jax.random.split(jax.random.key(seed), 7)
    queries = draw_queries(jax.random.fold_in(arg_keys[6], 71), 0)
    keys_in = draw_keys_in(jax.random.fold_in(arg_keys[6], 71), 0)
    values_in = bell_draw(arg_keys[2], (TOKENS, KVH * HD), 1.0, 6.0, ((0, 32),))
    cotangent = bell_draw(arg_keys[3], (TOKENS, H * HD), 1.0, 6.0, ((0, 32),))
    rand_blocks = draw_rand_blocks(jax.random.fold_in(arg_keys[6], 71), 0)
    glob_blocks = jax.random.randint(arg_keys[5], (NG,), 0, NB).astype(jnp.int32)
    return dict(queries=queries, keys_in=keys_in, values_in=values_in, cotangent=cotangent, rand_blocks=rand_blocks, glob_blocks=glob_blocks)


def reference(queries, keys_in, values_in, cotangent, rand_blocks, glob_blocks):
    total_rows = queries.shape[0]
    block_count = total_rows // BLK
    group_size = H // KVH
    scale_factor = 1.0 / math.sqrt(HD)
    highest = lax.Precision.HIGHEST
    block_ids = jnp.arange(block_count, dtype=jnp.int32)
    window_ids = block_ids[:, None] + jnp.arange(-1, 2, dtype=jnp.int32)[None, :]
    window_ok = (window_ids >= 0) & (window_ids < block_count)
    glob_ids = jnp.broadcast_to(glob_blocks.astype(jnp.int32)[None, :], (block_count, NG))
    key_ids = jnp.concatenate([jnp.clip(window_ids, 0, block_count - 1), glob_ids, rand_blocks.astype(jnp.int32)], axis=1)
    slot_ok = jnp.concatenate([window_ok, jnp.ones((block_count, NG + NR), jnp.bool_)], axis=1)
    key_mask = jnp.repeat(slot_ok, BLK, axis=1)
    query_all = queries.reshape(total_rows, H, HD)
    dout_all = cotangent.reshape(total_rows, H, HD)
    keys_all = keys_in.reshape(total_rows, KVH, HD)
    values_all = values_in.reshape(total_rows, KVH, HD)

    def one_head(head_id):
        kv_group = head_id // group_size
        query_rows = lax.dynamic_index_in_dim(query_all, head_id, 1, keepdims=False).astype(jnp.float32).reshape(block_count, BLK, HD)
        dout_rows = lax.dynamic_index_in_dim(dout_all, head_id, 1, keepdims=False).astype(jnp.float32).reshape(block_count, BLK, HD)
        key_rows = lax.dynamic_index_in_dim(keys_all, kv_group, 1, keepdims=False).astype(jnp.float32).reshape(block_count, BLK, HD)
        value_rows = lax.dynamic_index_in_dim(values_all, kv_group, 1, keepdims=False).astype(jnp.float32).reshape(block_count, BLK, HD)
        key_sets = key_rows[key_ids].reshape(block_count, NK * BLK, HD)
        value_sets = value_rows[key_ids].reshape(block_count, NK * BLK, HD)
        scores = jnp.einsum('nqd,nkd->nqk', query_rows, key_sets, precision=highest) * scale_factor
        scores = jnp.where(key_mask[:, None, :], scores, -1e+30)
        row_max = lax.optimization_barrier(jnp.max(scores, axis=2, keepdims=True))
        weights = jnp.exp(scores - row_max)
        row_sum = lax.optimization_barrier(jnp.sum(weights, axis=2, keepdims=True))
        probs_full = weights / row_sum
        probs_low = probs_full.astype(jnp.bfloat16).astype(jnp.float32)
        attended = jnp.einsum('nqk,nkd->nqd', probs_low, value_sets, precision=highest).astype(jnp.bfloat16)
        dprobs = jnp.einsum('nqd,nkd->nqk', dout_rows, value_sets, precision=highest)
        centre = lax.optimization_barrier(jnp.sum(probs_full * dprobs, axis=2, keepdims=True))
        dscores = (probs_full * (dprobs - centre)).astype(jnp.bfloat16).astype(jnp.float32)
        dquery = (jnp.einsum('nqk,nkd->nqd', dscores, key_sets, precision=highest) * scale_factor).astype(jnp.bfloat16)
        key_grads = jnp.einsum('nqk,nqd->nkd', dscores, query_rows, precision=highest) * scale_factor
        value_grads = jnp.einsum('nqk,nqd->nkd', probs_low, dout_rows, precision=highest)
        pair_terms = jnp.concatenate([key_grads, value_grads], axis=2).reshape(block_count, NK, BLK, 2 * HD)
        near_terms = pair_terms[:, :3 + NG]
        far_terms = lax.optimization_barrier(pair_terms[:, 3 + NG:].astype(jnp.bfloat16)).astype(jnp.float32)
        all_terms = jnp.concatenate([near_terms, far_terms], axis=1).reshape(block_count * NK, BLK, 2 * HD)
        totals = jnp.zeros((block_count, BLK, 2 * HD), jnp.float32).at[key_ids.reshape(-1)].add(all_terms)
        return (attended.reshape(total_rows, HD), dquery.reshape(total_rows, HD), totals.reshape(total_rows, 2 * HD).astype(jnp.bfloat16))
    attended_heads, dquery_heads, pair_heads = lax.map(one_head, jnp.arange(H, dtype=jnp.int32))
    attn_out = jnp.transpose(attended_heads, (1, 0, 2)).reshape(total_rows, H * HD)
    grad_query = jnp.transpose(dquery_heads, (1, 0, 2)).reshape(total_rows, H * HD)
    pair_sum = lax.optimization_barrier(jnp.sum(pair_heads.astype(jnp.float32).reshape(KVH, group_size, total_rows, 2 * HD), axis=1)).astype(jnp.bfloat16)
    pair_sum = jnp.transpose(pair_sum, (1, 0, 2))
    grad_keys = pair_sum[:, :, :HD].reshape(total_rows, KVH * HD)
    grad_values = pair_sum[:, :, HD:].reshape(total_rows, KVH * HD)
    return (attn_out, grad_query, grad_keys, grad_values)
```

```python
import functools
import math

import jax
import jax.numpy as jnp
from jax import lax
from jax.experimental import pallas as pl
from jax.experimental.pallas import tpu as pltpu
from jax.sharding import PartitionSpec as P

HD = 128
H = 32
KVH = 4
BLK = 128
NG = 2
GROUP = H // KVH
SCALE = 1.0 / math.sqrt(HD)
NEG_FILL = -1e30
AXES = ("ctx", "heads")
FAR = 1 + NG
SLOTS = 3 + FAR
WIDE = GROUP * BLK
PAIR = 2 * BLK
BF16 = jnp.bfloat16
F32 = jnp.float32

NT = (((1,), (1,)), ((), ()))


def params(mib, **kw):
    return pltpu.CompilerParams(vmem_limit_bytes=mib << 20, **kw)


def all_to_all(value):
    return lax.all_to_all(value, AXES, split_axis=0, concat_axis=0, tiled=True)


def shifted(value, steps):
    heads, ctx = lax.axis_size("heads"), lax.axis_size("ctx")
    count = heads * ctx
    place = lambda block: (block % heads) * ctx + block // heads
    pairs = [
        (place(i), place(i + steps)) for i in range(count) if 0 <= i + steps < count
    ]
    return lax.ppermute(value, ("heads", "ctx"), pairs)


def pack_kernel(k_ref, v_ref, out_ref):
    for g in range(KVH):
        cols = slice(g * HD, (g + 1) * HD)
        out_ref[0, g] = k_ref[:, cols]
        out_ref[1, g] = v_ref[:, cols]


def pack(keys, values):
    return pl.pallas_call(
        pack_kernel,
        out_shape=jax.ShapeDtypeStruct((2, KVH, BLK, HD), BF16),
        compiler_params=params(8),
        name="pack",
    )(keys, values)


def select_kernel(rand_ref, glob_ref, in_ref, out_ref):
    count = in_ref.shape[0]
    globs = [in_ref[glob_ref[slot]] for slot in range(NG)]
    for i in range(count):
        out_ref[i, 0] = in_ref[rand_ref[i, 0]]
        for slot in range(NG):
            out_ref[i, 1 + slot] = globs[slot]


def select(rand_blocks, glob_blocks, slices):
    count, rows, _ = slices.shape
    if rows % 16:
        rand_part = slices[rand_blocks[:, 0]]
        glob_part = jnp.broadcast_to(slices[glob_blocks][None], (count, NG, rows, HD))
        return jnp.concatenate([rand_part[:, None], glob_part], axis=1)
    return pl.pallas_call(
        select_kernel,
        out_shape=jax.ShapeDtypeStruct((count, FAR, rows, HD), BF16),
        in_specs=[
            pl.BlockSpec(memory_space=pltpu.SMEM),
            pl.BlockSpec(memory_space=pltpu.SMEM),
            pl.BlockSpec(memory_space=pltpu.VMEM),
        ],
        out_specs=pl.BlockSpec(memory_space=pltpu.VMEM),
        compiler_params=params(8),
        name="select",
    )(rand_blocks, glob_blocks, slices)


def combine_kernel(rand_ref, glob_ref, in_ref, out_ref, acc_ref):
    count = in_ref.shape[0]
    acc_ref[...] = jnp.zeros_like(acc_ref)
    for slot in range(NG):
        total = in_ref[0, 1 + slot].astype(F32)
        for i in range(1, count):
            total = total + in_ref[i, 1 + slot].astype(F32)
        acc_ref[glob_ref[slot]] += total
    for i in range(count):
        acc_ref[rand_ref[i, 0]] += in_ref[i, 0].astype(F32)
    out_ref[...] = acc_ref[...].astype(BF16)


def combine(rand_blocks, glob_blocks, terms):
    count, _, rows, _ = terms.shape
    if rows % 16:
        wide = terms.astype(F32)
        total = jnp.zeros((count, rows, HD), F32)
        total = total.at[glob_blocks].add(jnp.sum(wide[:, 1:], axis=0))
        return total.at[rand_blocks[:, 0]].add(wide[:, 0]).astype(BF16)
    return pl.pallas_call(
        combine_kernel,
        out_shape=jax.ShapeDtypeStruct((count, rows, HD), BF16),
        in_specs=[
            pl.BlockSpec(memory_space=pltpu.SMEM),
            pl.BlockSpec(memory_space=pltpu.SMEM),
            pl.BlockSpec(memory_space=pltpu.VMEM),
        ],
        out_specs=pl.BlockSpec(memory_space=pltpu.VMEM),
        scratch_shapes=[pltpu.VMEM((count, rows, HD), F32)],
        compiler_params=params(16),
        name="combine",
    )(rand_blocks, glob_blocks, terms)


def stacked(ref):
    return jnp.concatenate(
        [ref[:, h * HD : (h + 1) * HD] for h in range(GROUP)], axis=0
    )


def keys_of(kind, own_ref, left_ref, right_ref, far_ref):
    blocks = [left_ref[kind, 0], own_ref[kind, 0], right_ref[kind, 0]]
    for slot in (1, 2, 0):
        blocks.append(far_ref[kind, :, slot].reshape(BLK, HD))
    return blocks


def scores_kernel(
    edge_ref, q_ref, do_ref, own_ref, left_ref, right_ref, far_ref,
    probs_ref, ds_ref, terms_ref, s_ref, dp_ref,
):
    keys = keys_of(0, own_ref, left_ref, right_ref, far_ref)
    values = keys_of(1, own_ref, left_ref, right_ref, far_ref)
    queries, douts = stacked(q_ref), stacked(do_ref)
    factor = SCALE / math.log(2.0)
    for pair in range(WIDE // PAIR):
        cols = slice(pair * PAIR, (pair + 1) * PAIR)
        q, do = queries[cols], douts[cols]
        row_max = None
        for b in range(SLOTS):
            s = lax.dot_general(keys[b], q, NT, preferred_element_type=F32)
            if b == 0:
                s = jnp.where(edge_ref[0] == 0, s, NEG_FILL)
            if b == 2:
                s = jnp.where(edge_ref[1] == 0, s, NEG_FILL)
            s_ref[b * BLK : (b + 1) * BLK] = s
            top = jnp.max(s, axis=0, keepdims=True)
            row_max = top if row_max is None else jnp.maximum(row_max, top)
        row_sum = jnp.zeros((1, PAIR), F32)
        centre = jnp.zeros((1, PAIR), F32)
        for b in range(SLOTS):
            rows = slice(b * BLK, (b + 1) * BLK)
            w = jnp.exp2((s_ref[rows] - row_max) * factor)
            dp = lax.dot_general(values[b], do, NT, preferred_element_type=F32)
            s_ref[rows] = w
            dp_ref[rows] = dp
            row_sum = row_sum + jnp.sum(w, axis=0, keepdims=True)
            centre = centre + jnp.sum(w * dp, axis=0, keepdims=True)
        inverse = 1.0 / row_sum
        centre = centre * inverse
        for b in range(SLOTS):
            rows = slice(b * BLK, (b + 1) * BLK)
            p = s_ref[rows] * inverse
            probs_ref[0, rows, cols] = p.astype(BF16)
            ds_ref[0, rows, cols] = (p * (dp_ref[rows] - centre)).astype(BF16)
    share = terms_ref.shape[1]
    for slot, b in enumerate((5, 3, 4)):
        rows = slice(b * BLK, (b + 1) * BLK)
        dk = jnp.dot(ds_ref[0, rows], queries, preferred_element_type=F32) * SCALE
        dv = jnp.dot(probs_ref[0, rows], douts, preferred_element_type=F32)
        terms_ref[0, :, slot] = dk.astype(BF16).reshape(share, BLK // share, HD)
        terms_ref[1, :, slot] = dv.astype(BF16).reshape(share, BLK // share, HD)


def outputs_kernel(
    q_ref, do_ref, own_ref, left_ref, right_ref, far_ref, probs_ref, ds_ref,
    out_ref, dq_ref, to_left_ref, to_right_ref, near_ref,
):
    keys_t = jnp.concatenate(
        [k.T for k in keys_of(0, own_ref, left_ref, right_ref, far_ref)], axis=1
    )
    values_t = jnp.concatenate(
        [v.T for v in keys_of(1, own_ref, left_ref, right_ref, far_ref)], axis=1
    )
    for pair in range(WIDE // PAIR):
        cols = slice(pair * PAIR, (pair + 1) * PAIR)
        out_t = jnp.dot(values_t, probs_ref[0, :, cols], preferred_element_type=F32)
        dq_t = jnp.dot(keys_t, ds_ref[0, :, cols], preferred_element_type=F32) * SCALE
        for half in range(2):
            part = slice(half * HD, (half + 1) * HD)
            dest = slice(pair * PAIR + half * HD, pair * PAIR + (half + 1) * HD)
            out_ref[:, dest] = out_t[:, part].T.astype(BF16)
            dq_ref[:, dest] = dq_t[:, part].T.astype(BF16)
    queries, douts = stacked(q_ref), stacked(do_ref)
    for b, dest in enumerate((to_left_ref, near_ref, to_right_ref)):
        rows = slice(b * BLK, (b + 1) * BLK)
        dk = jnp.dot(ds_ref[0, rows], queries, preferred_element_type=F32) * SCALE
        dv = jnp.dot(probs_ref[0, rows], douts, preferred_element_type=F32)
        dest[0, 0] = dk.astype(dest.dtype)
        dest[1, 0] = dv.astype(dest.dtype)


def finish_kernel(near_ref, left_ref, right_ref, far_ref, dk_ref, dv_ref):
    for kind, dest in enumerate((dk_ref, dv_ref)):
        for g in range(KVH):
            total = near_ref[kind, g] + left_ref[kind, g].astype(F32)
            total = total + right_ref[kind, g].astype(F32)
            total = total + far_ref[kind, g].astype(F32)
            dest[:, g * HD : (g + 1) * HD] = total.astype(BF16)


def finish(near, left, right, far):
    shape = jax.ShapeDtypeStruct((BLK, KVH * HD), BF16)
    return pl.pallas_call(
        finish_kernel,
        out_shape=(shape, shape),
        compiler_params=params(8),
        name="finish",
    )(near, left, right, far)


def group_specs(share):
    token = pl.BlockSpec((BLK, WIDE), lambda g, *_: (0, g))
    block = pl.BlockSpec((2, 1, BLK, HD), lambda g, *_: (0, g, 0, 0))
    far = pl.BlockSpec(
        (2, share, FAR, BLK // share, HD), lambda g, *_: (0, g, 0, 0, 0)
    )
    square = pl.BlockSpec((1, SLOTS * BLK, WIDE), lambda g, *_: (g, 0, 0))
    return token, block, far, square


def shards(queries, keys_in, values_in, cotangent, rand_blocks, glob_blocks):
    heads, ctx = lax.axis_size("heads"), lax.axis_size("ctx")
    count = heads * ctx
    mine = lax.axis_index("ctx") * heads + lax.axis_index("heads")
    edges = jnp.array([mine == 0, mine == count - 1]).astype(jnp.int32)
    rows = 2 * KVH * BLK // count
    packed = pack(keys_in, values_in)
    slices = all_to_all(packed.reshape(count, rows, HD))
    left = shifted(packed, 1)
    right = shifted(packed, -1)
    far = all_to_all(select(rand_blocks, glob_blocks, slices))
    if rows % 16:
        share = 1
        far = jnp.transpose(
            far.reshape(2, KVH, BLK // rows, FAR, rows, HD), (0, 1, 3, 2, 4, 5)
        )
    else:
        share = BLK // rows
    far = far.reshape(2, KVH * share, FAR, BLK // share, HD)
    token, block, far_spec, square = group_specs(share)
    square_shape = jax.ShapeDtypeStruct((KVH, SLOTS * BLK, WIDE), BF16)
    block_shape = jax.ShapeDtypeStruct((2, KVH, BLK, HD), BF16)
    flops = 2 * H * BLK * SLOTS * BLK * HD
    probs, ds, terms = pl.pallas_call(
        scores_kernel,
        grid_spec=pltpu.PrefetchScalarGridSpec(
            num_scalar_prefetch=1,
            grid=(KVH,),
            in_specs=[token, token, block, block, block, far_spec],
            out_specs=[square, square, far_spec],
            scratch_shapes=[pltpu.VMEM((SLOTS * BLK, PAIR), F32)] * 2,
        ),
        out_shape=(
            square_shape,
            square_shape,
            jax.ShapeDtypeStruct(far.shape, BF16),
        ),
        compiler_params=params(32, dimension_semantics=("arbitrary",)),
        cost_estimate=pl.CostEstimate(
            flops=3 * flops, bytes_accessed=16 << 20, transcendentals=H * BLK * SLOTS * BLK
        ),
        name="scores",
    )(edges, queries, cotangent, packed, left, right, far)
    if rows % 16:
        terms = jnp.transpose(
            terms.reshape(2, KVH, FAR, BLK // rows, rows, HD), (0, 1, 3, 2, 4, 5)
        )
    arrived = all_to_all(terms.reshape(count, FAR, rows, HD))
    token_shape = jax.ShapeDtypeStruct(queries.shape, BF16)
    attn_out, grad_query, to_left, to_right, near = pl.pallas_call(
        outputs_kernel,
        grid=(KVH,),
        in_specs=[token, token, block, block, block, far_spec, square, square],
        out_specs=[token, token, block, block, block],
        out_shape=(
            token_shape,
            token_shape,
            block_shape,
            block_shape,
            jax.ShapeDtypeStruct((2, KVH, BLK, HD), F32),
        ),
        compiler_params=params(32, dimension_semantics=("arbitrary",)),
        cost_estimate=pl.CostEstimate(
            flops=3 * flops, bytes_accessed=18 << 20, transcendentals=0
        ),
        name="outputs",
    )(queries, cotangent, packed, left, right, far, probs, ds)
    from_right = shifted(to_left, -1)
    from_left = shifted(to_right, 1)
    summed = combine(rand_blocks, glob_blocks, arrived)
    returned = all_to_all(summed).reshape(2, KVH, BLK, HD)
    grad_keys, grad_values = finish(near, from_left, from_right, returned)
    return attn_out, grad_query, grad_keys, grad_values


def solution(mesh):
    spec = P(AXES, None)
    return jax.shard_map(
        shards,
        mesh=mesh,
        in_specs=(spec, spec, spec, spec, P(), P()),
        out_specs=(spec, spec, spec, spec),
        check_vma=False,
    )
```

```python
import functools
import math

import jax
import jax.numpy as jnp
from jax import lax
from jax.experimental import pallas as pl
from jax.experimental.pallas import tpu as pltpu
from jax.sharding import PartitionSpec as P

HD = 128
H = 32
KVH = 4
BLK = 128
NG = 2
GROUP = H // KVH
SCALE = 1.0 / math.sqrt(HD)
NEG_FILL = -1e30
AXES = ("ctx", "heads")
FAR = 1 + NG
SLOTS = 3 + FAR
WIDE = GROUP * BLK
PAIR = 2 * BLK
BF16 = jnp.bfloat16
F32 = jnp.float32

NT = (((1,), (1,)), ((), ()))


def params(mib, **kw):
    return pltpu.CompilerParams(vmem_limit_bytes=mib << 20, **kw)


def all_to_all(value):
    return lax.all_to_all(value, AXES, split_axis=0, concat_axis=0, tiled=True)


def shifted(value, steps):
    heads, ctx = lax.axis_size("heads"), lax.axis_size("ctx")
    count = heads * ctx
    place = lambda block: (block % heads) * ctx + block // heads
    pairs = [
        (place(i), place(i + steps)) for i in range(count) if 0 <= i + steps < count
    ]
    return lax.ppermute(value, ("heads", "ctx"), pairs)


def pack_kernel(k_ref, v_ref, out_ref):
    for g in range(KVH):
        cols = slice(g * HD, (g + 1) * HD)
        out_ref[0, g] = k_ref[:, cols]
        out_ref[1, g] = v_ref[:, cols]


def pack(keys, values):
    return pl.pallas_call(
        pack_kernel,
        out_shape=jax.ShapeDtypeStruct((2, KVH, BLK, HD), BF16),
        compiler_params=params(8),
        name="pack",
    )(keys, values)


def select_kernel(rand_ref, glob_ref, in_ref, out_ref):
    count = in_ref.shape[0]
    globs = [in_ref[glob_ref[slot]] for slot in range(NG)]
    for i in range(count):
        out_ref[i, 0] = in_ref[rand_ref[i, 0]]
        for slot in range(NG):
            out_ref[i, 1 + slot] = globs[slot]


def select(rand_blocks, glob_blocks, slices):
    count, rows, _ = slices.shape
    if rows % 16:
        rand_part = slices[rand_blocks[:, 0]]
        glob_part = jnp.broadcast_to(slices[glob_blocks][None], (count, NG, rows, HD))
        return jnp.concatenate([rand_part[:, None], glob_part], axis=1)
    return pl.pallas_call(
        select_kernel,
        out_shape=jax.ShapeDtypeStruct((count, FAR, rows, HD), BF16),
        in_specs=[
            pl.BlockSpec(memory_space=pltpu.SMEM),
            pl.BlockSpec(memory_space=pltpu.SMEM),
            pl.BlockSpec(memory_space=pltpu.VMEM),
        ],
        out_specs=pl.BlockSpec(memory_space=pltpu.VMEM),
        compiler_params=params(8),
        name="select",
    )(rand_blocks, glob_blocks, slices)


def combine_kernel(rand_ref, glob_ref, in_ref, out_ref, acc_ref):
    count = in_ref.shape[0]
    acc_ref[...] = jnp.zeros_like(acc_ref)
    for slot in range(NG):
        total = in_ref[0, 1 + slot].astype(F32)
        for i in range(1, count):
            total = total + in_ref[i, 1 + slot].astype(F32)
        acc_ref[glob_ref[slot]] += total
    for i in range(count):
        acc_ref[rand_ref[i, 0]] += in_ref[i, 0].astype(F32)
    out_ref[...] = acc_ref[...].astype(BF16)


def combine(rand_blocks, glob_blocks, terms):
    count, _, rows, _ = terms.shape
    if rows % 16:
        wide = terms.astype(F32)
        total = jnp.zeros((count, rows, HD), F32)
        total = total.at[glob_blocks].add(jnp.sum(wide[:, 1:], axis=0))
        return total.at[rand_blocks[:, 0]].add(wide[:, 0]).astype(BF16)
    return pl.pallas_call(
        combine_kernel,
        out_shape=jax.ShapeDtypeStruct((count, rows, HD), BF16),
        in_specs=[
            pl.BlockSpec(memory_space=pltpu.SMEM),
            pl.BlockSpec(memory_space=pltpu.SMEM),
            pl.BlockSpec(memory_space=pltpu.VMEM),
        ],
        out_specs=pl.BlockSpec(memory_space=pltpu.VMEM),
        scratch_shapes=[pltpu.VMEM((count, rows, HD), F32)],
        compiler_params=params(16),
        name="combine",
    )(rand_blocks, glob_blocks, terms)


def stacked(ref):
    return jnp.concatenate(
        [ref[:, h * HD : (h + 1) * HD] for h in range(GROUP)], axis=0
    )


def keys_of(kind, own_ref, left_ref, right_ref, far_ref):
    blocks = [left_ref[kind, 0], own_ref[kind, 0], right_ref[kind, 0]]
    for slot in (1, 2, 0):
        blocks.append(far_ref[kind, :, slot].reshape(BLK, HD))
    return blocks


def scores_kernel(
    edge_ref, q_ref, do_ref, own_ref, left_ref, right_ref, far_ref,
    probs_ref, ds_ref, terms_ref, s_ref, dp_ref,
):
    keys = keys_of(0, own_ref, left_ref, right_ref, far_ref)
    values = keys_of(1, own_ref, left_ref, right_ref, far_ref)
    queries, douts = stacked(q_ref), stacked(do_ref)
    factor = SCALE / math.log(2.0)
    for pair in range(WIDE // PAIR):
        cols = slice(pair * PAIR, (pair + 1) * PAIR)
        q, do = queries[cols], douts[cols]
        row_max = None
        for b in range(SLOTS):
            s = lax.dot_general(keys[b], q, NT, preferred_element_type=F32)
            if b == 0:
                s = jnp.where(edge_ref[0] == 0, s, NEG_FILL)
            if b == 2:
                s = jnp.where(edge_ref[1] == 0, s, NEG_FILL)
            s_ref[b * BLK : (b + 1) * BLK] = s
            top = jnp.max(s, axis=0, keepdims=True)
            row_max = top if row_max is None else jnp.maximum(row_max, top)
        row_sum = jnp.zeros((1, PAIR), F32)
        centre = jnp.zeros((1, PAIR), F32)
        for b in range(SLOTS):
            rows = slice(b * BLK, (b + 1) * BLK)
            w = jnp.exp2((s_ref[rows] - row_max) * factor)
            dp = lax.dot_general(values[b], do, NT, preferred_element_type=F32)
            s_ref[rows] = w
            dp_ref[rows] = dp
            row_sum = row_sum + jnp.sum(w, axis=0, keepdims=True)
            centre = centre + jnp.sum(w * dp, axis=0, keepdims=True)
        inverse = 1.0 / row_sum
        centre = centre * inverse
        for b in range(SLOTS):
            rows = slice(b * BLK, (b + 1) * BLK)
            p = s_ref[rows] * inverse
            probs_ref[0, rows, cols] = p.astype(BF16)
            ds_ref[0, rows, cols] = (p * (dp_ref[rows] - centre)).astype(BF16)
    share = terms_ref.shape[1]
    for slot, b in enumerate((5, 3, 4)):
        rows = slice(b * BLK, (b + 1) * BLK)
        dk = jnp.dot(ds_ref[0, rows], queries, preferred_element_type=F32) * SCALE
        dv = jnp.dot(probs_ref[0, rows], douts, preferred_element_type=F32)
        terms_ref[0, :, slot] = dk.astype(BF16).reshape(share, BLK // share, HD)
        terms_ref[1, :, slot] = dv.astype(BF16).reshape(share, BLK // share, HD)


def outputs_kernel(
    q_ref, do_ref, own_ref, left_ref, right_ref, far_ref, probs_ref, ds_ref,
    out_ref, dq_ref, to_left_ref, to_right_ref, near_ref,
):
    keys_t = jnp.concatenate(
        [k.T for k in keys_of(0, own_ref, left_ref, right_ref, far_ref)], axis=1
    )
    values_t = jnp.concatenate(
        [v.T for v in keys_of(1, own_ref, left_ref, right_ref, far_ref)], axis=1
    )
    for pair in range(WIDE // PAIR):
        cols = slice(pair * PAIR, (pair + 1) * PAIR)
        out_t = jnp.dot(values_t, probs_ref[0, :, cols], preferred_element_type=F32)
        dq_t = jnp.dot(keys_t, ds_ref[0, :, cols], preferred_element_type=F32) * SCALE
        for half in range(2):
            part = slice(half * HD, (half + 1) * HD)
            dest = slice(pair * PAIR + half * HD, pair * PAIR + (half + 1) * HD)
            out_ref[:, dest] = out_t[:, part].T.astype(BF16)
            dq_ref[:, dest] = dq_t[:, part].T.astype(BF16)
    queries, douts = stacked(q_ref), stacked(do_ref)
    for b, dest in enumerate((to_left_ref, near_ref, to_right_ref)):
        rows = slice(b * BLK, (b + 1) * BLK)
        dk = jnp.dot(ds_ref[0, rows], queries, preferred_element_type=F32) * SCALE
        dv = jnp.dot(probs_ref[0, rows], douts, preferred_element_type=F32)
        dest[0, 0] = dk.astype(dest.dtype)
        dest[1, 0] = dv.astype(dest.dtype)


def finish_kernel(near_ref, left_ref, right_ref, far_ref, dk_ref, dv_ref):
    for kind, dest in enumerate((dk_ref, dv_ref)):
        for g in range(KVH):
            total = near_ref[kind, g] + left_ref[kind, g].astype(F32)
            total = total + right_ref[kind, g].astype(F32)
            total = total + far_ref[kind, g].astype(F32)
            dest[:, g * HD : (g + 1) * HD] = total.astype(BF16)


def finish(near, left, right, far):
    shape = jax.ShapeDtypeStruct((BLK, KVH * HD), BF16)
    return pl.pallas_call(
        finish_kernel,
        out_shape=(shape, shape),
        compiler_params=params(8),
        name="finish",
    )(near, left, right, far)


def group_specs(share):
    token = pl.BlockSpec((BLK, WIDE), lambda g, *_: (0, g))
    block = pl.BlockSpec((2, 1, BLK, HD), lambda g, *_: (0, g, 0, 0))
    far = pl.BlockSpec(
        (2, share, FAR, BLK // share, HD), lambda g, *_: (0, g, 0, 0, 0)
    )
    square = pl.BlockSpec((1, SLOTS * BLK, WIDE), lambda g, *_: (g, 0, 0))
    return token, block, far, square


def shards(queries, keys_in, values_in, cotangent, rand_blocks, glob_blocks):
    heads, ctx = lax.axis_size("heads"), lax.axis_size("ctx")
    count = heads * ctx
    mine = lax.axis_index("ctx") * heads + lax.axis_index("heads")
    edges = jnp.array([mine == 0, mine == count - 1]).astype(jnp.int32)
    rows = 2 * KVH * BLK // count
    packed = pack(keys_in, values_in)
    slices = all_to_all(packed.reshape(count, rows, HD))
    left = shifted(packed, 1)
    right = shifted(packed, -1)
    far = all_to_all(select(rand_blocks, glob_blocks, slices))
    if rows % 16:
        share = 1
        far = jnp.transpose(
            far.reshape(2, KVH, BLK // rows, FAR, rows, HD), (0, 1, 3, 2, 4, 5)
        )
    else:
        share = BLK // rows
    far = far.reshape(2, KVH * share, FAR, BLK // share, HD)
    token, block, far_spec, square = group_specs(share)
    square_shape = jax.ShapeDtypeStruct((KVH, SLOTS * BLK, WIDE), BF16)
    block_shape = jax.ShapeDtypeStruct((2, KVH, BLK, HD), BF16)
    flops = 2 * H * BLK * SLOTS * BLK * HD
    probs, ds, terms = pl.pallas_call(
        scores_kernel,
        grid_spec=pltpu.PrefetchScalarGridSpec(
            num_scalar_prefetch=1,
            grid=(KVH,),
            in_specs=[token, token, block, block, block, far_spec],
            out_specs=[square, square, far_spec],
            scratch_shapes=[pltpu.VMEM((SLOTS * BLK, PAIR), F32)] * 2,
        ),
        out_shape=(
            square_shape,
            square_shape,
            jax.ShapeDtypeStruct(far.shape, BF16),
        ),
        compiler_params=params(56, dimension_semantics=("arbitrary",)),
        cost_estimate=pl.CostEstimate(
            flops=3 * flops, bytes_accessed=16 << 20, transcendentals=H * BLK * SLOTS * BLK
        ),
        name="scores",
    )(edges, queries, cotangent, packed, left, right, far)
    if rows % 16:
        terms = jnp.transpose(
            terms.reshape(2, KVH, FAR, BLK // rows, rows, HD), (0, 1, 3, 2, 4, 5)
        )
    arrived = all_to_all(terms.reshape(count, FAR, rows, HD))
    token_shape = jax.ShapeDtypeStruct(queries.shape, BF16)
    attn_out, grad_query, to_left, to_right, near = pl.pallas_call(
        outputs_kernel,
        grid=(KVH,),
        in_specs=[token, token, block, block, block, far_spec, square, square],
        out_specs=[token, token, block, block, block],
        out_shape=(
            token_shape,
            token_shape,
            block_shape,
            block_shape,
            jax.ShapeDtypeStruct((2, KVH, BLK, HD), F32),
        ),
        compiler_params=params(56, dimension_semantics=("arbitrary",)),
        cost_estimate=pl.CostEstimate(
            flops=3 * flops, bytes_accessed=18 << 20, transcendentals=0
        ),
        name="outputs",
    )(queries, cotangent, packed, left, right, far, probs, ds)
    arrived, to_left, to_right = lax.optimization_barrier((arrived, to_left, to_right))
    from_right = shifted(to_left, -1)
    from_left = shifted(to_right, 1)
    summed = combine(rand_blocks, glob_blocks, arrived)
    returned = all_to_all(summed).reshape(2, KVH, BLK, HD)
    grad_keys, grad_values = finish(near, from_left, from_right, returned)
    return attn_out, grad_query, grad_keys, grad_values


def solution(mesh):
    spec = P(AXES, None)
    return jax.shard_map(
        shards,
        mesh=mesh,
        in_specs=(spec, spec, spec, spec, P(), P()),
        out_specs=(spec, spec, spec, spec),
        check_vma=False,
    )
```

```python
import math

import jax
import jax.numpy as jnp
from jax import lax
from jax.experimental import pallas as pl
from jax.experimental.pallas import tpu as pltpu
from jax.sharding import PartitionSpec as P

HD = 128
H = 32
KVH = 4
BLK = 128
NG = 2
GROUP = H // KVH
SCALE = 1.0 / math.sqrt(HD)
NEG_FILL = -1e30
AXES = ("ctx", "heads")
MATES = 2
GL = KVH // MATES
FAR = MATES + NG
SLOTS = 3 + NG + 1
WIDE = GROUP * BLK
PAIR = 2 * BLK
HALF_ROWS = 2 * GL * BLK
BF16 = jnp.bfloat16
F32 = jnp.float32
NT = (((1,), (1,)), ((), ()))


def params(mib, **kw):
    return pltpu.CompilerParams(vmem_limit_bytes=mib << 20, **kw)


def all_to_all(value):
    return lax.all_to_all(value, AXES, split_axis=0, concat_axis=0, tiled=True)


def mate(value):
    count = lax.axis_size("ctx")
    return lax.ppermute(value, "ctx", [(i, i ^ 1) for i in range(count)])


def neighbour_pairs(step, of_mate):
    heads, ctx = lax.axis_size("heads"), lax.axis_size("ctx")
    pairs = []
    for c in range(ctx):
        for h in range(heads):
            block = (c ^ 1 if of_mate else c) * heads + h + step
            if 0 <= block < heads * ctx:
                source = (block // heads) & ~1 | c & 1
                pairs.append(((block % heads) * ctx + source, h * ctx + c))
    return pairs


def permute(value, pairs):
    return lax.ppermute(value, ("heads", "ctx"), pairs)


def swap(pairs):
    return [(j, i) for i, j in pairs]


MATE, LEFT, RIGHT, LAST, FIRST, CORE = 0, 1, 3, 5, 6, 7


def table_of():
    heads, ctx = lax.axis_size("heads"), lax.axis_size("ctx")
    h, c = lax.axis_index("heads"), lax.axis_index("ctx")
    own, other = c * heads + h, (c ^ 1) * heads + h
    last = heads * ctx - 1
    flags = [
        c & 1,
        own == 0,
        other == 0,
        own == last,
        other == last,
        h == heads - 1,
        h == 0,
    ]
    return jnp.stack([jnp.asarray(f).astype(jnp.int32) for f in flags])


def pack_kernel(k_ref, v_ref, out_ref):
    share = out_ref.shape[0] // (2 * GL)
    for kind, ref in enumerate((k_ref, v_ref)):
        for half in range(MATES):
            for g in range(GL):
                first = (kind * GL + g) * share
                column = (half * GL + g) * HD
                out_ref[first : first + share, half] = ref[
                    :, column : column + HD
                ].reshape(share, BLK // share, HD)


def pack(keys, values, count):
    rows = HALF_ROWS // count
    if rows % 16:
        both = jnp.stack([keys, values]).reshape(2, BLK, MATES, GL, HD)
        both = jnp.transpose(both, (0, 3, 1, 2, 4)).reshape(count, rows, MATES, HD)
        return jnp.transpose(both, (0, 2, 1, 3))
    return pl.pallas_call(
        pack_kernel,
        out_shape=jax.ShapeDtypeStruct((count, MATES, rows, HD), BF16),
        compiler_params=params(8),
        name="pack",
    )(keys, values)


def side_of(i, heads):
    return (i // heads) % MATES


def mate_of(i, heads):
    return (i // heads ^ 1) * heads + i % heads


def select_kernel(heads, table_ref, in_ref, out_ref):
    count = in_ref.shape[0]
    for i in range(count):
        side = side_of(i, heads)
        out_ref[i, 0] = in_ref[table_ref[i], side]
        out_ref[i, 1] = in_ref[table_ref[mate_of(i, heads)], side]
        for slot in range(NG):
            out_ref[i, MATES + slot] = in_ref[table_ref[count + slot], side]


def select(wanted, slices, heads):
    count, _, rows, _ = slices.shape
    if rows % 16:
        i = jnp.arange(count)
        blocks = jnp.stack(
            [wanted[i], wanted[mate_of(i, heads)]]
            + [jnp.broadcast_to(wanted[count + slot], (count,)) for slot in range(NG)],
            axis=1,
        )
        return slices[blocks, side_of(i, heads)[:, None]]
    return pl.pallas_call(
        lambda *refs: select_kernel(heads, *refs),
        out_shape=jax.ShapeDtypeStruct((count, FAR, rows, HD), BF16),
        in_specs=[
            pl.BlockSpec(memory_space=pltpu.SMEM),
            pl.BlockSpec(memory_space=pltpu.VMEM),
        ],
        out_specs=pl.BlockSpec(memory_space=pltpu.VMEM),
        compiler_params=params(8),
        name="select",
    )(wanted, slices)


def combine_kernel(heads, table_ref, in_ref, out_ref, acc_ref):
    count = in_ref.shape[0]
    acc_ref[...] = jnp.zeros_like(acc_ref)
    for slot in range(NG):
        for side in range(MATES):
            total = None
            for i in range(count):
                if side_of(i, heads) == side:
                    term = in_ref[i, MATES + slot].astype(F32)
                    total = term if total is None else total + term
            acc_ref[table_ref[count + slot], side] += total
    for i in range(count):
        side = side_of(i, heads)
        acc_ref[table_ref[i], side] += in_ref[i, 0].astype(F32)
        acc_ref[table_ref[mate_of(i, heads)], side] += in_ref[i, 1].astype(F32)
    out_ref[...] = acc_ref[...].astype(BF16)


def combine(wanted, terms, heads):
    count, _, rows, _ = terms.shape
    if rows % 16:
        i = jnp.arange(count)
        side = side_of(i, heads)
        wide = terms.astype(F32)
        total = jnp.zeros((count, MATES, rows, HD), F32)
        total = total.at[wanted[i], side].add(wide[:, 0])
        total = total.at[wanted[mate_of(i, heads)], side].add(wide[:, 1])
        for slot in range(NG):
            block = jnp.broadcast_to(wanted[count + slot], (count,))
            total = total.at[block, side].add(wide[:, MATES + slot])
        return total.astype(BF16)
    return pl.pallas_call(
        lambda *refs: combine_kernel(heads, *refs),
        out_shape=jax.ShapeDtypeStruct((count, MATES, rows, HD), BF16),
        in_specs=[
            pl.BlockSpec(memory_space=pltpu.SMEM),
            pl.BlockSpec(memory_space=pltpu.VMEM),
        ],
        out_specs=pl.BlockSpec(memory_space=pltpu.VMEM),
        scratch_shapes=[pltpu.VMEM((count, MATES, rows, HD), F32)],
        compiler_params=params(16),
        name="combine",
    )(wanted, terms)


def send_kernel(table_ref, k_ref, v_ref, mk_ref, mv_ref, *out_refs):
    first = table_ref[MATE] * GL
    for g in range(GL):
        cols = pl.ds(pl.multiple_of((first + g) * HD, HD), HD)
        for kind, (own, other) in enumerate(((k_ref, mk_ref), (v_ref, mv_ref))):
            a, b = own[:, cols], other[:, cols]
            for flag, dest in ((LAST, 0), (FIRST, 2)):
                crossed = table_ref[flag] != 0
                out_refs[dest][kind, g] = jnp.where(crossed, b, a)
                out_refs[dest + 1][kind, g] = jnp.where(crossed, a, b)


def send(table, keys, values, mate_keys, mate_values):
    shape = jax.ShapeDtypeStruct((2, GL, BLK, HD), BF16)
    vmem = pl.BlockSpec(memory_space=pltpu.VMEM)
    return pl.pallas_call(
        send_kernel,
        out_shape=(shape,) * 4,
        in_specs=[pl.BlockSpec(memory_space=pltpu.SMEM)] + [vmem] * 4,
        out_specs=(vmem,) * 4,
        compiler_params=params(8),
        name="send",
    )(table, keys, values, mate_keys, mate_values)


def stacked(value):
    return jnp.concatenate(
        [value[:, h * HD : (h + 1) * HD] for h in range(GROUP)], axis=0
    )


def chosen(s, own, other):
    return jnp.where(s == 0, own, other)


def blocks_of(kind, s, own, other, left, mate_left, right, mate_right, far_ref):
    blocks = [
        chosen(s, left[kind, 0], mate_left[kind, 0]),
        chosen(s, own[...], other[...]),
        chosen(s, right[kind, 0], mate_right[kind, 0]),
    ]
    for slot in range(NG):
        blocks.append(far_ref[kind, 0, :, MATES + slot].reshape(BLK, HD))
    blocks.append(far_ref[kind, 0, :, s].reshape(BLK, HD))
    return blocks


def grads_of(b, queries, douts, probs_ref, ds_ref):
    rows = slice(b * BLK, (b + 1) * BLK)
    dk = jnp.dot(ds_ref[0, 0, rows], queries, preferred_element_type=F32) * SCALE
    dv = jnp.dot(probs_ref[0, 0, rows], douts, preferred_element_type=F32)
    return dk, dv


def scores_kernel(
    table_ref, q_ref, mq_ref, do_ref, mdo_ref, k_ref, mk_ref, v_ref, mv_ref,
    left, mate_left, right, mate_right, far_ref,
    probs_ref, ds_ref, terms_ref, s_ref, dp_ref, glob_ref,
):
    s = pl.program_id(1)
    near = (left, mate_left, right, mate_right, far_ref)
    keys = blocks_of(0, s, k_ref, mk_ref, *near)
    values = blocks_of(1, s, v_ref, mv_ref, *near)
    queries = stacked(chosen(s, q_ref[...], mq_ref[...]))
    douts = stacked(chosen(s, do_ref[...], mdo_ref[...]))
    outside = {0: table_ref[LEFT + s] != 0, 2: table_ref[RIGHT + s] != 0}
    factor = SCALE / math.log(2.0)
    for pair in range(WIDE // PAIR):
        cols = slice(pair * PAIR, (pair + 1) * PAIR)
        q, do = queries[cols], douts[cols]
        row_max = None
        for b in range(SLOTS):
            score = lax.dot_general(keys[b], q, NT, preferred_element_type=F32)
            if b in outside:
                score = jnp.where(outside[b], NEG_FILL, score)
            s_ref[b * BLK : (b + 1) * BLK] = score
            top = jnp.max(score, axis=0, keepdims=True)
            row_max = top if row_max is None else jnp.maximum(row_max, top)
        row_sum = jnp.zeros((1, PAIR), F32)
        centre = jnp.zeros((1, PAIR), F32)
        for b in range(SLOTS):
            rows = slice(b * BLK, (b + 1) * BLK)
            w = jnp.exp2((s_ref[rows] - row_max) * factor)
            dp = lax.dot_general(values[b], do, NT, preferred_element_type=F32)
            s_ref[rows] = w
            dp_ref[rows] = dp
            row_sum = row_sum + jnp.sum(w, axis=0, keepdims=True)
            centre = centre + jnp.sum(w * dp, axis=0, keepdims=True)
        inverse = 1.0 / row_sum
        centre = centre * inverse
        for b in range(SLOTS):
            rows = slice(b * BLK, (b + 1) * BLK)
            p = s_ref[rows] * inverse
            probs_ref[0, 0, rows, cols] = p.astype(BF16)
            ds_ref[0, 0, rows, cols] = (p * (dp_ref[rows] - centre)).astype(BF16)
    share = terms_ref.shape[2]

    def put(slot, pair):
        for kind, term in enumerate(pair):
            terms_ref[kind, 0, :, slot] = term.astype(BF16).reshape(
                share, BLK // share, HD
            )

    put(s, grads_of(5, queries, douts, probs_ref, ds_ref))
    globs = [grads_of(3 + slot, queries, douts, probs_ref, ds_ref) for slot in range(NG)]

    @pl.when(s == 0)
    def _():
        for slot in range(NG):
            for kind in range(2):
                glob_ref[slot, kind] = globs[slot][kind]

    @pl.when(s == 1)
    def _():
        for slot in range(NG):
            put(MATES + slot, [globs[slot][kind] + glob_ref[slot, kind] for kind in range(2)])


def outputs_kernel(
    table_ref, q_ref, mq_ref, do_ref, mdo_ref, k_ref, mk_ref, v_ref, mv_ref,
    left, mate_left, right, mate_right, far_ref, probs_ref, ds_ref,
    out_ref, mate_out_ref, dq_ref, mate_dq_ref,
    to_left, mate_to_left, to_right, mate_to_right, near_ref, both_ref,
):
    s = pl.program_id(1)
    near = (left, mate_left, right, mate_right, far_ref)
    keys_t, values_t = (
        jnp.concatenate([x.T for x in blocks_of(kind, s, own, other, *near)], axis=1)
        for kind, own, other in ((0, k_ref, mk_ref), (1, v_ref, mv_ref))
    )
    for pair in range(WIDE // PAIR):
        cols = slice(pair * PAIR, (pair + 1) * PAIR)
        out_t = jnp.dot(values_t, probs_ref[0, 0, :, cols], preferred_element_type=F32)
        dq_t = jnp.dot(keys_t, ds_ref[0, 0, :, cols], preferred_element_type=F32) * SCALE
        for half in range(2):
            part = slice(half * HD, (half + 1) * HD)
            dest = slice(pair * PAIR + half * HD, pair * PAIR + (half + 1) * HD)
            both_ref[0, :, dest] = out_t[:, part].T.astype(BF16)
            both_ref[1, :, dest] = dq_t[:, part].T.astype(BF16)
    queries = stacked(chosen(s, q_ref[...], mq_ref[...]))
    douts = stacked(chosen(s, do_ref[...], mdo_ref[...]))
    terms = [grads_of(b, queries, douts, probs_ref, ds_ref) for b in range(3)]
    for kind in range(2):
        near_ref[0, kind, 0] = terms[1][kind]

    def write(out, dq, to_left, to_right):
        out[...] = both_ref[0]
        dq[...] = both_ref[1]
        for kind in range(2):
            to_left[kind, 0] = terms[0][kind].astype(BF16)
            to_right[kind, 0] = terms[2][kind].astype(BF16)

    @pl.when(s == 0)
    def _():
        write(out_ref, dq_ref, to_left, to_right)

    @pl.when(s == 1)
    def _():
        write(mate_out_ref, mate_dq_ref, mate_to_left, mate_to_right)


def merge_kernel(table_ref, near_ref, lo, lm, ro, rm, own_ref, other_ref):
    last, first = table_ref[LAST] != 0, table_ref[FIRST] != 0
    a, b, c, d = (ref[...].astype(F32) for ref in (lo, lm, ro, rm))
    own_ref[...] = near_ref[0] + jnp.where(last, b, a) + jnp.where(first, d, c)
    other_ref[...] = near_ref[1] + jnp.where(last, a, b) + jnp.where(first, c, d)


def merge(table, near, terms):
    shape = jax.ShapeDtypeStruct((2, GL, BLK, HD), F32)
    vmem = pl.BlockSpec(memory_space=pltpu.VMEM)
    return pl.pallas_call(
        merge_kernel,
        out_shape=(shape, shape),
        in_specs=[pl.BlockSpec(memory_space=pltpu.SMEM)] + [vmem] * 5,
        out_specs=(vmem, vmem),
        compiler_params=params(16),
        name="merge",
    )(table, near, *terms)


def finish_kernel(table_ref, own_ref, other_ref, far_ref, dk_ref, dv_ref):
    mine = table_ref[MATE]
    share = far_ref.shape[2]
    for kind, dest in enumerate((dk_ref, dv_ref)):
        for half in range(MATES):
            for g in range(GL):
                near = jnp.where(mine == half, own_ref[kind, g], other_ref[kind, g])
                far = far_ref[kind, g, :, half].reshape(BLK, HD).astype(F32)
                column = (half * GL + g) * HD
                dest[:, column : column + HD] = (near + far).astype(BF16)


def finish(table, own, other, far):
    shape = jax.ShapeDtypeStruct((BLK, KVH * HD), BF16)
    vmem = pl.BlockSpec(memory_space=pltpu.VMEM)
    return pl.pallas_call(
        finish_kernel,
        out_shape=(shape, shape),
        in_specs=[pl.BlockSpec(memory_space=pltpu.SMEM)] + [vmem] * 3,
        out_specs=(vmem, vmem),
        compiler_params=params(8),
        name="finish",
    )(table, own, other, far)


def shards(queries, keys_in, values_in, cotangent, rand_blocks, glob_blocks):
    heads = lax.axis_size("heads")
    count = heads * lax.axis_size("ctx")
    rows = HALF_ROWS // count
    plain = rows % 16 == 0
    share = BLK // rows if plain else 1
    table = table_of()
    wanted = jnp.concatenate([rand_blocks[:, 0], glob_blocks])

    slices = all_to_all(pack(keys_in, values_in, count))
    mate_keys, mate_values = mate(keys_in), mate(values_in)
    mate_queries, mate_cotangent = mate(queries), mate(cotangent)
    sent = send(table, keys_in, values_in, mate_keys, mate_values)
    routes = [neighbour_pairs(step, of_mate) for step in (-1, 1) for of_mate in (False, True)]
    near = [permute(value, pairs) for value, pairs in zip(sent, routes)]
    far = all_to_all(select(wanted, slices, heads))
    if not plain:
        far = far.reshape(2, GL, BLK // rows, FAR, rows, HD)
        far = jnp.transpose(far, (0, 1, 3, 2, 4, 5))
    far = far.reshape(2, GL, share, FAR, BLK // share, HD)

    token = pl.BlockSpec((BLK, WIDE), lambda g, s, t: (0, t[MATE] * GL + g))
    token_half = pl.BlockSpec((BLK, WIDE), lambda g, s, t: (0, g))
    key = pl.BlockSpec((BLK, HD), lambda g, s, t: (0, t[MATE] * GL + g))
    block = pl.BlockSpec((2, 1, BLK, HD), lambda g, s, t: (0, g, 0, 0))
    far_spec = pl.BlockSpec(
        (2, 1, share, FAR, BLK // share, HD), lambda g, s, t: (0, g, 0, 0, 0, 0)
    )
    square = pl.BlockSpec((1, 1, SLOTS * BLK, WIDE), lambda g, s, t: (g, s, 0, 0))
    square_shape = jax.ShapeDtypeStruct((GL, MATES, SLOTS * BLK, WIDE), BF16)
    block_shape = jax.ShapeDtypeStruct((2, GL, BLK, HD), BF16)
    token_shape = jax.ShapeDtypeStruct(queries.shape, BF16)
    half_shape = jax.ShapeDtypeStruct((BLK, GL * WIDE), BF16)
    flops = 2 * H * BLK * SLOTS * BLK * HD
    operands = (
        table, queries, mate_queries, cotangent, mate_cotangent,
        keys_in, mate_keys, values_in, mate_values, *near, far,
    )
    in_specs = [token] * 4 + [key] * 4 + [block] * 4 + [far_spec]
    order = ("arbitrary", "arbitrary")
    probs, ds, terms = pl.pallas_call(
        scores_kernel,
        grid_spec=pltpu.PrefetchScalarGridSpec(
            num_scalar_prefetch=1,
            grid=(GL, MATES),
            in_specs=in_specs,
            out_specs=[square, square, far_spec],
            scratch_shapes=[pltpu.VMEM((SLOTS * BLK, PAIR), F32)] * 2
            + [pltpu.VMEM((NG, 2, BLK, HD), F32)],
        ),
        out_shape=(square_shape, square_shape, jax.ShapeDtypeStruct(far.shape, BF16)),
        compiler_params=params(56, dimension_semantics=order),
        cost_estimate=pl.CostEstimate(
            flops=3 * flops, bytes_accessed=16 << 20, transcendentals=H * BLK * SLOTS * BLK
        ),
        name="scores",
    )(*operands)
    if not plain:
        terms = jnp.transpose(
            terms.reshape(2, GL, FAR, BLK // rows, rows, HD), (0, 1, 3, 2, 4, 5)
        )
    arrived = all_to_all(terms.reshape(count, FAR, rows, HD))
    near_spec = pl.BlockSpec((1, 2, 1, BLK, HD), lambda g, s, t: (s, 0, g, 0, 0))
    out, mate_out, dq, mate_dq, *back, near_grads = pl.pallas_call(
        outputs_kernel,
        grid_spec=pltpu.PrefetchScalarGridSpec(
            num_scalar_prefetch=1,
            grid=(GL, MATES),
            in_specs=in_specs + [square, square],
            out_specs=[token, token_half, token, token_half] + [block] * 4 + [near_spec],
            scratch_shapes=[pltpu.VMEM((2, BLK, WIDE), BF16)],
        ),
        out_shape=(token_shape, half_shape, token_shape, half_shape)
        + (block_shape,) * 4
        + (jax.ShapeDtypeStruct((MATES, 2, GL, BLK, HD), F32),),
        compiler_params=params(56, dimension_semantics=order),
        cost_estimate=pl.CostEstimate(
            flops=3 * flops, bytes_accessed=18 << 20, transcendentals=0
        ),
        name="outputs",
    )(*operands, probs, ds)
    back = [permute(value, swap(pairs)) for value, pairs in zip(back, routes)]
    other_column = (1 - table[MATE]) * (GL * WIDE)
    attn_out = lax.dynamic_update_slice(out, mate(mate_out), (0, other_column))
    grad_query = lax.dynamic_update_slice(dq, mate(mate_dq), (0, other_column))
    arrived, *back = lax.optimization_barrier((arrived, *back))
    own_grads, mate_grads = merge(table, near_grads, back)
    other_grads = mate(mate_grads)
    returned = all_to_all(combine(wanted, arrived, heads))
    if not plain:
        returned = returned.reshape(2, GL, BLK // rows, MATES, rows, HD)
        returned = jnp.transpose(returned, (0, 1, 3, 2, 4, 5))
    returned = returned.reshape(2, GL, share, MATES, BLK // share, HD)
    grad_keys, grad_values = finish(table, own_grads, other_grads, returned)
    return attn_out, grad_query, grad_keys, grad_values


def solution(mesh):
    spec = P(AXES, None)
    return jax.shard_map(
        shards,
        mesh=mesh,
        in_specs=(spec, spec, spec, spec, P(), P()),
        out_specs=(spec, spec, spec, spec),
        check_vma=False,
    )
```

```python
import math

import jax
import jax.numpy as jnp
from jax import lax
from jax.experimental import pallas as pl
from jax.experimental.pallas import tpu as pltpu
from jax.sharding import PartitionSpec as P

HD = 128
H = 32
KVH = 4
BLK = 128
NG = 2
GROUP = H // KVH
SCALE = 1.0 / math.sqrt(HD)
NEG_FILL = -1e30
AXES = ("ctx", "heads")
MATES = 2
SLOTS = 3 + NG + 1
WIDE = GROUP * BLK
PAIR = 2 * BLK
BF16 = jnp.bfloat16
F32 = jnp.float32

NT = (((1,), (1,)), ((), ()))


def params(mib, **kw):
    return pltpu.CompilerParams(vmem_limit_bytes=mib << 20, **kw)


def all_to_all(value):
    return lax.all_to_all(value, AXES, split_axis=0, concat_axis=0, tiled=True)


def mate(value):
    count = lax.axis_size("ctx")
    return lax.ppermute(value, "ctx", [(i, i ^ 1) for i in range(count)])


def swap_inner(value):
    heads = lax.axis_size("heads")
    return lax.ppermute(value, "heads", [(h, h ^ 1) for h in range(heads)])


def swap_outer(value):
    heads, ctx = lax.axis_size("heads"), lax.axis_size("ctx")
    pairs = []
    for i in range(1, heads * ctx - 1):
        j = i + 1 if i % 2 else i - 1
        pairs.append(tuple(b % heads * ctx + b // heads for b in (i, j)))
    return lax.ppermute(value, ("heads", "ctx"), pairs)


def pack_kernel(k_ref, v_ref, out_ref):
    for g in range(KVH):
        cols = slice(g * HD, (g + 1) * HD)
        out_ref[0, g] = k_ref[:, cols]
        out_ref[1, g] = v_ref[:, cols]


def pack(keys, values):
    return pl.pallas_call(
        pack_kernel,
        out_shape=jax.ShapeDtypeStruct((2, KVH, BLK, HD), BF16),
        compiler_params=params(58),
        name="pack",
    )(keys, values)


def side_of(i, heads):
    return i // heads % MATES


def select_kernel(heads, wanted_ref, in_ref, out_ref):
    count = in_ref.shape[0]
    globs = [in_ref[wanted_ref[count + slot]] for slot in range(NG)]
    for i in range(count):
        out_ref[i, 0] = in_ref[wanted_ref[i]]
        out_ref[i, 1] = globs[side_of(i, heads)]


def select(wanted, slices, heads):
    count, rows, _ = slices.shape
    if rows % 16:
        i = jnp.arange(count)
        glob = wanted[count + side_of(i, heads)]
        return slices[jnp.stack([wanted[i], glob], axis=1)]
    return pl.pallas_call(
        lambda *refs: select_kernel(heads, *refs),
        out_shape=jax.ShapeDtypeStruct((count, 2, rows, HD), BF16),
        in_specs=[
            pl.BlockSpec(memory_space=pltpu.SMEM),
            pl.BlockSpec(memory_space=pltpu.VMEM),
        ],
        out_specs=pl.BlockSpec(memory_space=pltpu.VMEM),
        compiler_params=params(8),
        name="select",
    )(wanted, slices)


def combine_kernel(heads, wanted_ref, in_ref, out_ref, acc_ref):
    count = in_ref.shape[0]
    acc_ref[...] = jnp.zeros_like(acc_ref)
    for side in range(MATES):
        total = None
        for i in range(count):
            if side_of(i, heads) == side:
                term = in_ref[i, 1].astype(F32)
                total = term if total is None else total + term
        acc_ref[wanted_ref[count + side]] += total
    for i in range(count):
        acc_ref[wanted_ref[i]] += in_ref[i, 0].astype(F32)
    out_ref[...] = acc_ref[...].astype(BF16)


def combine(wanted, terms, heads):
    count, _, rows, _ = terms.shape
    if rows % 16:
        i = jnp.arange(count)
        wide = terms.astype(F32)
        total = jnp.zeros((count, rows, HD), F32).at[wanted[i]].add(wide[:, 0])
        return total.at[wanted[count + side_of(i, heads)]].add(wide[:, 1]).astype(BF16)
    return pl.pallas_call(
        lambda *refs: combine_kernel(heads, *refs),
        out_shape=jax.ShapeDtypeStruct((count, rows, HD), BF16),
        in_specs=[
            pl.BlockSpec(memory_space=pltpu.SMEM),
            pl.BlockSpec(memory_space=pltpu.VMEM),
        ],
        out_specs=pl.BlockSpec(memory_space=pltpu.VMEM),
        scratch_shapes=[pltpu.VMEM((count, rows, HD), F32)],
        compiler_params=params(16),
        name="combine",
    )(wanted, terms)


def join_kernel(random_ref, glob_ref, other_ref, out_ref):
    out_ref[:, 0] = random_ref[...]
    out_ref[:, 1] = (glob_ref[...] + other_ref[...].astype(F32)).astype(BF16)


def join(random, glob, other):
    count, rows, _ = random.shape
    if rows % 16:
        total = (glob + other.astype(F32)).astype(BF16)
        return jnp.stack([random, total], axis=1)
    return pl.pallas_call(
        join_kernel,
        out_shape=jax.ShapeDtypeStruct((count, 2, rows, HD), BF16),
        compiler_params=params(58),
        name="join",
    )(random, glob, other)


def stacked(ref):
    return jnp.concatenate(
        [ref[:, h * HD : (h + 1) * HD] for h in range(GROUP)], axis=0
    )


def blocks_of(kind, own_ref, inner_ref, outer_ref, far_ref, other_ref):
    blocks = [inner_ref[kind, 0], outer_ref[kind, 0], own_ref[kind, 0]]
    for ref, slot in ((far_ref, 1), (other_ref, 1), (far_ref, 0)):
        blocks.append(ref[kind, :, slot].reshape(BLK, HD))
    return blocks


def grads_of(b, queries, douts, probs_ref, ds_ref):
    rows = slice(b * BLK, (b + 1) * BLK)
    dk = jnp.dot(ds_ref[0, rows], queries, preferred_element_type=F32) * SCALE
    dv = jnp.dot(probs_ref[0, rows], douts, preferred_element_type=F32)
    return dk, dv


def scores_kernel(
    edge_ref, q_ref, do_ref, own_ref, inner_ref, outer_ref, far_ref, other_ref,
    probs_ref, ds_ref, random_ref, glob_ref, mate_ref, s_ref, dp_ref,
):
    near = (own_ref, inner_ref, outer_ref, far_ref, other_ref)
    keys, values = blocks_of(0, *near), blocks_of(1, *near)
    queries, douts = stacked(q_ref), stacked(do_ref)
    factor = SCALE / math.log(2.0)
    for pair in range(WIDE // PAIR):
        cols = slice(pair * PAIR, (pair + 1) * PAIR)
        q, do = queries[cols], douts[cols]
        row_max = None
        for b in range(SLOTS):
            s = lax.dot_general(keys[b], q, NT, preferred_element_type=F32)
            if b == 1:
                s = jnp.where(edge_ref[0] == 0, s, NEG_FILL)
            s_ref[b * BLK : (b + 1) * BLK] = s
            top = jnp.max(s, axis=0, keepdims=True)
            row_max = top if row_max is None else jnp.maximum(row_max, top)
        row_sum = jnp.zeros((1, PAIR), F32)
        centre = jnp.zeros((1, PAIR), F32)
        for b in range(SLOTS):
            rows = slice(b * BLK, (b + 1) * BLK)
            w = jnp.exp2((s_ref[rows] - row_max) * factor)
            dp = lax.dot_general(values[b], do, NT, preferred_element_type=F32)
            s_ref[rows] = w
            dp_ref[rows] = dp
            row_sum = row_sum + jnp.sum(w, axis=0, keepdims=True)
            centre = centre + jnp.sum(w * dp, axis=0, keepdims=True)
        inverse = 1.0 / row_sum
        centre = centre * inverse
        for b in range(SLOTS):
            rows = slice(b * BLK, (b + 1) * BLK)
            p = s_ref[rows] * inverse
            probs_ref[0, rows, cols] = p.astype(BF16)
            ds_ref[0, rows, cols] = (p * (dp_ref[rows] - centre)).astype(BF16)
    for b, dest in ((4, mate_ref), (3, glob_ref), (5, random_ref)):
        for kind, term in enumerate(grads_of(b, queries, douts, probs_ref, ds_ref)):
            dest[kind, 0] = term.astype(dest.dtype)


def window_kernel(q_ref, do_ref, probs_ref, ds_ref, inner_ref, outer_ref):
    queries, douts = stacked(q_ref), stacked(do_ref)
    for b, dest in enumerate((inner_ref, outer_ref)):
        for kind, term in enumerate(grads_of(b, queries, douts, probs_ref, ds_ref)):
            dest[kind, 0] = term.astype(BF16)


def outputs_kernel(
    q_ref, do_ref, own_ref, inner_ref, outer_ref, far_ref, other_ref, probs_ref, ds_ref,
    from_inner_ref, from_outer_ref, out_ref, dq_ref, near_ref,
):
    near = (own_ref, inner_ref, outer_ref, far_ref, other_ref)
    keys_t, values_t = (
        jnp.concatenate([x.T for x in blocks_of(kind, *near)], axis=1)
        for kind in range(2)
    )
    for pair in range(WIDE // PAIR):
        cols = slice(pair * PAIR, (pair + 1) * PAIR)
        out_t = jnp.dot(values_t, probs_ref[0, :, cols], preferred_element_type=F32)
        dq_t = jnp.dot(keys_t, ds_ref[0, :, cols], preferred_element_type=F32) * SCALE
        for half in range(2):
            part = slice(half * HD, (half + 1) * HD)
            dest = slice(pair * PAIR + half * HD, pair * PAIR + (half + 1) * HD)
            out_ref[:, dest] = out_t[:, part].T.astype(BF16)
            dq_ref[:, dest] = dq_t[:, part].T.astype(BF16)
    queries, douts = stacked(q_ref), stacked(do_ref)
    for kind, term in enumerate(grads_of(2, queries, douts, probs_ref, ds_ref)):
        back = from_inner_ref[kind, 0].astype(F32) + from_outer_ref[kind, 0].astype(F32)
        near_ref[kind, 0] = term + back


def finish_kernel(near_ref, far_ref, dk_ref, dv_ref):
    for kind, dest in enumerate((dk_ref, dv_ref)):
        for g in range(KVH):
            total = near_ref[kind, g] + far_ref[kind, g].astype(F32)
            dest[:, g * HD : (g + 1) * HD] = total.astype(BF16)


def finish(near, far):
    shape = jax.ShapeDtypeStruct((BLK, KVH * HD), BF16)
    return pl.pallas_call(
        finish_kernel,
        out_shape=(shape, shape),
        compiler_params=params(8),
        name="finish",
    )(near, far)


def shards(queries, keys_in, values_in, cotangent, rand_blocks, glob_blocks):
    heads, ctx = lax.axis_size("heads"), lax.axis_size("ctx")
    count = heads * ctx
    mine = lax.axis_index("ctx") * heads + lax.axis_index("heads")
    edges = ((mine == 0) | (mine == count - 1)).astype(jnp.int32).reshape(1)
    wanted = jnp.concatenate([rand_blocks[:, 0], glob_blocks])
    rows = 2 * KVH * BLK // count
    share = BLK // rows if rows % 16 == 0 else 1
    packed = pack(keys_in, values_in)
    slices = all_to_all(packed.reshape(count, rows, HD))
    inner, outer = swap_inner(packed), swap_outer(packed)
    slices, inner = lax.optimization_barrier((slices, inner))
    far = all_to_all(select(wanted, slices, heads))
    far, outer = lax.optimization_barrier((far, outer))
    if share == 1:
        far = far.reshape(2, KVH, BLK // rows, 2, rows, HD)
        far = jnp.transpose(far, (0, 1, 3, 2, 4, 5))
    far = far.reshape(2, KVH * share, 2, BLK // share, HD)
    other = mate(far)

    token = pl.BlockSpec((BLK, WIDE), lambda g, *_: (0, g))
    block = pl.BlockSpec((2, 1, BLK, HD), lambda g, *_: (0, g, 0, 0))
    far_spec = pl.BlockSpec((2, share, 2, BLK // share, HD), lambda g, *_: (0, g, 0, 0, 0))
    square = pl.BlockSpec((1, SLOTS * BLK, WIDE), lambda g, *_: (g, 0, 0))
    two_rows = pl.BlockSpec((1, 2 * BLK, WIDE), lambda g, *_: (g, 0, 0))
    square_shape = jax.ShapeDtypeStruct((KVH, SLOTS * BLK, WIDE), BF16)
    token_shape = jax.ShapeDtypeStruct(queries.shape, BF16)
    low, wide = (jax.ShapeDtypeStruct((2, KVH, BLK, HD), dtype) for dtype in (BF16, F32))
    flops = 2 * H * BLK * SLOTS * BLK * HD
    blocks = (packed, inner, outer, far, other)
    block_specs = [block] * 3 + [far_spec] * 2

    def call(kernel, name, work, in_specs, outs, scalars=0, scratch=()):
        return pl.pallas_call(
            kernel,
            grid_spec=pltpu.PrefetchScalarGridSpec(
                num_scalar_prefetch=scalars,
                grid=(KVH,),
                in_specs=[token, token] + in_specs,
                out_specs=[spec for spec, _ in outs],
                scratch_shapes=scratch,
            ),
            out_shape=[shape for _, shape in outs],
            compiler_params=params(56, dimension_semantics=("arbitrary",)),
            cost_estimate=pl.CostEstimate(
                flops=work * flops, bytes_accessed=16 << 20, transcendentals=0
            ),
            name=name,
        )

    probs, ds, random, glob, for_mate = call(
        scores_kernel,
        "scores",
        3,
        block_specs,
        [(square, square_shape)] * 2 + [(block, low), (block, wide), (block, low)],
        1,
        [pltpu.VMEM((SLOTS * BLK, PAIR), F32)] * 2,
    )(edges, queries, cotangent, *blocks)
    flat = (count, rows, HD)
    terms = join(random.reshape(flat), glob.reshape(flat), mate(for_mate).reshape(flat))
    arrived = all_to_all(terms)
    back = call(
        window_kernel, "window", 1, [two_rows, two_rows], [(block, low)] * 2
    )(queries, cotangent, probs, ds)
    back = [swap_inner(back[0]), swap_outer(back[1])]
    arrived, *back = lax.optimization_barrier((arrived, *back))
    summed = combine(wanted, arrived, heads)
    returned = all_to_all(summed).reshape(2, KVH, BLK, HD)
    probs, summed = lax.optimization_barrier((probs, summed))
    attn_out, grad_query, near = call(
        outputs_kernel,
        "outputs",
        2,
        block_specs + [square, square, block, block],
        [(token, token_shape)] * 2 + [(block, wide)],
    )(queries, cotangent, *blocks, probs, ds, *back)
    grad_keys, grad_values = finish(near, returned)
    return attn_out, grad_query, grad_keys, grad_values


def solution(mesh):
    spec = P(AXES, None)
    return jax.shard_map(
        shards,
        mesh=mesh,
        in_specs=(spec, spec, spec, spec, P(), P()),
        out_specs=(spec, spec, spec, spec),
        check_vma=False,
    )
```

```python
import math

import jax
import jax.numpy as jnp
from jax import lax
from jax.experimental import pallas as pl
from jax.experimental.pallas import tpu as pltpu
from jax.sharding import PartitionSpec as P

HD = 128
H = 32
KVH = 4
BLK = 128
NG = 2
GROUP = H // KVH
SCALE = 1.0 / math.sqrt(HD)
NEG_FILL = -1e30
AXES = ("ctx", "heads")
MATES = 2
SLOTS = 3 + NG + 1
WIDE = GROUP * BLK
PART = WIDE
FACTOR = SCALE / math.log(2.0)
BF16 = jnp.bfloat16
F32 = jnp.float32

NT = (((1,), (1,)), ((), ()))


def params(mib, **kw):
    return pltpu.CompilerParams(vmem_limit_bytes=mib << 20, **kw)


def all_to_all(value):
    return lax.all_to_all(value, AXES, split_axis=0, concat_axis=0, tiled=True)


def mate(value):
    count = lax.axis_size("ctx")
    return lax.ppermute(value, "ctx", [(i, i ^ 1) for i in range(count)])


def swap_inner(value):
    heads = lax.axis_size("heads")
    return lax.ppermute(value, "heads", [(h, h ^ 1) for h in range(heads)])


def swap_outer(value):
    heads, ctx = lax.axis_size("heads"), lax.axis_size("ctx")
    pairs = []
    for i in range(1, heads * ctx - 1):
        j = i + 1 if i % 2 else i - 1
        pairs.append(tuple(b % heads * ctx + b // heads for b in (i, j)))
    return lax.ppermute(value, ("heads", "ctx"), pairs)


def pack_kernel(k_ref, v_ref, out_ref):
    for g in range(KVH):
        cols = slice(g * HD, (g + 1) * HD)
        out_ref[0, g] = k_ref[:, cols]
        out_ref[1, g] = v_ref[:, cols]


def pack(keys, values):
    return pl.pallas_call(
        pack_kernel,
        out_shape=jax.ShapeDtypeStruct((2, KVH, BLK, HD), BF16),
        compiler_params=params(58),
        name="pack",
    )(keys, values)


def side_of(i, heads):
    return i // heads % MATES


def select_kernel(heads, wanted_ref, in_ref, out_ref):
    count = in_ref.shape[0]
    globs = [in_ref[wanted_ref[count + slot]] for slot in range(NG)]
    for i in range(count):
        out_ref[i, 0] = in_ref[wanted_ref[i]]
        out_ref[i, 1] = globs[side_of(i, heads)]


def select(wanted, slices, heads):
    count, rows, _ = slices.shape
    if rows % 16:
        i = jnp.arange(count)
        glob = wanted[count + side_of(i, heads)]
        return slices[jnp.stack([wanted[i], glob], axis=1)]
    return pl.pallas_call(
        lambda *refs: select_kernel(heads, *refs),
        out_shape=jax.ShapeDtypeStruct((count, 2, rows, HD), BF16),
        in_specs=[
            pl.BlockSpec(memory_space=pltpu.SMEM),
            pl.BlockSpec(memory_space=pltpu.VMEM),
        ],
        out_specs=pl.BlockSpec(memory_space=pltpu.VMEM),
        compiler_params=params(8),
        name="select",
    )(wanted, slices)


def combine_kernel(heads, wanted_ref, in_ref, out_ref, acc_ref):
    count = in_ref.shape[0]
    acc_ref[...] = jnp.zeros_like(acc_ref)
    for side in range(MATES):
        total = None
        for i in range(count):
            if side_of(i, heads) == side:
                term = in_ref[i, 1].astype(F32)
                total = term if total is None else total + term
        acc_ref[wanted_ref[count + side]] += total
    for i in range(count):
        acc_ref[wanted_ref[i]] += in_ref[i, 0].astype(F32)
    out_ref[...] = acc_ref[...].astype(BF16)


def combine(wanted, terms, heads):
    count, _, rows, _ = terms.shape
    if rows % 16:
        i = jnp.arange(count)
        wide = terms.astype(F32)
        total = jnp.zeros((count, rows, HD), F32).at[wanted[i]].add(wide[:, 0])
        return total.at[wanted[count + side_of(i, heads)]].add(wide[:, 1]).astype(BF16)
    return pl.pallas_call(
        lambda *refs: combine_kernel(heads, *refs),
        out_shape=jax.ShapeDtypeStruct((count, rows, HD), BF16),
        in_specs=[
            pl.BlockSpec(memory_space=pltpu.SMEM),
            pl.BlockSpec(memory_space=pltpu.VMEM),
        ],
        out_specs=pl.BlockSpec(memory_space=pltpu.VMEM),
        scratch_shapes=[pltpu.VMEM((count, rows, HD), F32)],
        compiler_params=params(16),
        name="combine",
    )(wanted, terms)


def join_kernel(random_ref, glob_ref, other_ref, out_ref):
    out_ref[:, 0] = random_ref[...]
    out_ref[:, 1] = (glob_ref[...] + other_ref[...].astype(F32)).astype(BF16)


def join(random, glob, other):
    count, rows, _ = random.shape
    if rows % 16:
        total = (glob + other.astype(F32)).astype(BF16)
        return jnp.stack([random, total], axis=1)
    return pl.pallas_call(
        join_kernel,
        out_shape=jax.ShapeDtypeStruct((count, 2, rows, HD), BF16),
        compiler_params=params(8),
        name="join",
    )(random, glob, other)


def stacked(ref):
    return jnp.concatenate(
        [ref[:, h * HD : (h + 1) * HD] for h in range(GROUP)], axis=0
    )


def blocks_of(near, far_ref, other_ref):
    blocks = list(near)
    for ref, slot in ((far_ref, 1), (other_ref, 1), (far_ref, 0)):
        blocks.append(ref[:, slot].reshape(BLK, HD))
    return blocks


def dot_nt(a, b):
    return lax.dot_general(a, b, NT, preferred_element_type=F32)


def put_grads(rows, queries, douts, probs_ref, ds_ref, dests):
    dk = jnp.dot(ds_ref[rows], queries, preferred_element_type=F32) * SCALE
    dv = jnp.dot(probs_ref[rows], douts, preferred_element_type=F32)
    for i, dest in enumerate(dests):
        for kind, term in enumerate((dk, dv)):
            dest[kind] = term[i * BLK : (i + 1) * BLK].astype(dest.dtype)


def block_rows(b):
    return slice(b * BLK, (b + 1) * BLK)


def masked(edge_ref, b, scores):
    return jnp.where(edge_ref[0] == 0, scores, NEG_FILL) if b == 1 else scores


def scores_kernel(
    edge_ref, far_ref, other_ref, q_any, do_any, inner_any, outer_any, own_any,
    stats_ref, glob_ref, mate_ref, random_ref,
    s_ref, dp_ref, probs_ref, ds_ref, near_ref, tokens_ref, sem, token_sem,
):
    copies = [
        pltpu.make_async_copy(ref, near_ref.at[i], sem.at[i])
        for i, ref in enumerate((inner_any, outer_any, own_any))
    ]

    def token_copies(g):
        cols = pl.ds(pl.multiple_of(g * WIDE, WIDE), WIDE)
        return [
            pltpu.make_async_copy(
                ref.at[:, cols], tokens_ref.at[i, g], token_sem.at[i, g]
            )
            for i, ref in enumerate((q_any, do_any))
        ]

    for copy in copies:
        copy.start()
    for g in range(KVH):
        for copy in token_copies(g):
            copy.start()
    for copy in copies:
        copy.wait()
    share = far_ref.shape[1] // KVH

    def group(g, carry):
        for copy in token_copies(g):
            copy.wait()
        queries, douts = (stacked(tokens_ref.at[i, g]) for i in range(2))
        keys, values = (
            jnp.concatenate(
                blocks_of(
                    [near_ref[i, kind, g] for i in range(3)],
                    far_ref.at[kind, pl.ds(g * share, share)],
                    other_ref.at[kind, pl.ds(g * share, share)],
                ),
                axis=0,
            )
            for kind in range(2)
        )
        for part in range(WIDE // PART):
            cols = slice(part * PART, (part + 1) * PART)
            s = dot_nt(keys, queries[cols])
            dp_ref[...] = dot_nt(values, douts[cols])
            row_max = None
            for b in range(SLOTS):
                score = masked(edge_ref, b, s[block_rows(b)])
                s_ref[block_rows(b)] = score
                top = jnp.max(score, axis=0, keepdims=True)
                row_max = top if row_max is None else jnp.maximum(row_max, top)
            row_sum = jnp.zeros((1, PART), F32)
            centre = jnp.zeros((1, PART), F32)
            for b in range(SLOTS):
                w = jnp.exp2((s_ref[block_rows(b)] - row_max) * FACTOR)
                if b >= 3:
                    s_ref[block_rows(b)] = w
                row_sum = row_sum + jnp.sum(w, axis=0, keepdims=True)
                moved = w * dp_ref[block_rows(b)]
                centre = centre + jnp.sum(moved, axis=0, keepdims=True)
            inverse = 1.0 / row_sum
            centre = centre * inverse
            stats_ref[g, 0:1, cols] = row_max
            stats_ref[g, 1:2, cols] = inverse
            stats_ref[g, 2:3, cols] = centre
            for b in range(3, SLOTS):
                rows = block_rows(b)
                p = s_ref[rows] * inverse
                dest = block_rows(b - 3)
                probs_ref[dest, cols] = p.astype(BF16)
                ds_ref[dest, cols] = (p * (dp_ref[rows] - centre)).astype(BF16)
        dests = [ref.at[:, g] for ref in (glob_ref, mate_ref, random_ref)]
        put_grads(slice(None), queries, douts, probs_ref, ds_ref, dests)
        return carry

    lax.fori_loop(0, KVH, group, 0)


def again(edge_ref, first, keys, values, q, do, stats_ref, probs_ref, ds_ref, cols):
    row_max, inverse, centre = (stats_ref[0, i : i + 1, cols] for i in range(3))
    s, dp = dot_nt(keys, q), dot_nt(values, do)
    for b in range(keys.shape[0] // BLK):
        rows = block_rows(b)
        score = masked(edge_ref, first + b, s[rows])
        p = jnp.exp2((score - row_max) * FACTOR) * inverse
        probs_ref[rows, cols] = p.astype(BF16)
        ds_ref[rows, cols] = (p * (dp[rows] - centre)).astype(BF16)


def window_kernel(
    edge_ref, q_ref, do_ref, inner_ref, outer_ref, stats_ref,
    to_inner_ref, to_outer_ref, probs_ref, ds_ref,
):
    keys, values = (
        jnp.concatenate([inner_ref[kind, 0], outer_ref[kind, 0]], axis=0)
        for kind in range(2)
    )
    queries, douts = stacked(q_ref), stacked(do_ref)
    for part in range(WIDE // PART):
        cols = slice(part * PART, (part + 1) * PART)
        again(
            edge_ref, 0, keys, values, queries[cols], douts[cols],
            stats_ref, probs_ref, ds_ref, cols,
        )
    put_grads(
        slice(None), queries, douts, probs_ref, ds_ref,
        (to_inner_ref.at[:, 0], to_outer_ref.at[:, 0]),
    )


def outputs_kernel(
    edge_ref, q_ref, do_ref, own_ref, inner_ref, outer_ref, far_ref, other_ref,
    stats_ref, from_inner_ref, from_outer_ref, out_ref, dq_ref, near_ref, probs_ref, ds_ref,
):
    key_blocks, value_blocks = (
        blocks_of(
            [ref[kind, 0] for ref in (inner_ref, outer_ref, own_ref)],
            far_ref.at[kind],
            other_ref.at[kind],
        )
        for kind in range(2)
    )
    keys, values = (jnp.concatenate(x, axis=0) for x in (key_blocks, value_blocks))
    keys_t, values_t = (
        jnp.concatenate([x.T for x in blocks], axis=1)
        for blocks in (key_blocks, value_blocks)
    )
    queries, douts = stacked(q_ref), stacked(do_ref)
    for part in range(WIDE // PART):
        cols = slice(part * PART, (part + 1) * PART)
        again(
            edge_ref, 0, keys, values, queries[cols], douts[cols],
            stats_ref, probs_ref, ds_ref, cols,
        )
        out_t = jnp.dot(values_t, probs_ref[:, cols], preferred_element_type=F32)
        dq_t = jnp.dot(keys_t, ds_ref[:, cols], preferred_element_type=F32) * SCALE
        for i in range(PART // HD):
            place = slice(i * HD, (i + 1) * HD)
            dest = slice(part * PART + i * HD, part * PART + (i + 1) * HD)
            out_ref[:, dest] = out_t[:, place].T.astype(BF16)
            dq_ref[:, dest] = dq_t[:, place].T.astype(BF16)
    put_grads(block_rows(2), queries, douts, probs_ref, ds_ref, (near_ref.at[:, 0],))
    for kind in range(2):
        back = from_inner_ref[kind, 0].astype(F32) + from_outer_ref[kind, 0].astype(F32)
        near_ref[kind, 0] += back


def finish_kernel(near_ref, far_ref, dk_ref, dv_ref):
    for kind, dest in enumerate((dk_ref, dv_ref)):
        for g in range(KVH):
            total = near_ref[kind, g] + far_ref[kind, g].astype(F32)
            dest[:, g * HD : (g + 1) * HD] = total.astype(BF16)


def finish(near, far):
    shape = jax.ShapeDtypeStruct((BLK, KVH * HD), BF16)
    return pl.pallas_call(
        finish_kernel,
        out_shape=(shape, shape),
        compiler_params=params(8),
        name="finish",
    )(near, far)


def shards(queries, keys_in, values_in, cotangent, rand_blocks, glob_blocks):
    heads, ctx = lax.axis_size("heads"), lax.axis_size("ctx")
    count = heads * ctx
    mine = lax.axis_index("ctx") * heads + lax.axis_index("heads")
    edges = ((mine == 0) | (mine == count - 1)).astype(jnp.int32).reshape(1)
    wanted = jnp.concatenate([rand_blocks[:, 0], glob_blocks])
    rows = 2 * KVH * BLK // count
    share = BLK // rows if rows % 16 == 0 else 1
    token = pl.BlockSpec((BLK, WIDE), lambda g: (0, g))
    block = pl.BlockSpec((2, 1, BLK, HD), lambda g: (0, g, 0, 0))
    far_spec = pl.BlockSpec((2, share, 2, BLK // share, HD), lambda g: (0, g, 0, 0, 0))
    stat = pl.BlockSpec((1, 8, WIDE), lambda g: (g, 0, 0))
    vmem = pl.BlockSpec(memory_space=pltpu.VMEM)
    smem = pl.BlockSpec(memory_space=pltpu.SMEM)
    anywhere = pl.BlockSpec(memory_space=pl.ANY)
    low, wide = (jax.ShapeDtypeStruct((2, KVH, BLK, HD), dtype) for dtype in (BF16, F32))
    token_shape = jax.ShapeDtypeStruct(queries.shape, BF16)
    flops = 2 * H * BLK * SLOTS * BLK * HD

    def call(kernel, name, work, mib, ins, outs, scratch=(), **kw):
        return pl.pallas_call(
            kernel,
            in_specs=ins,
            out_specs=[spec for spec, _ in outs],
            out_shape=[shape for _, shape in outs],
            scratch_shapes=scratch,
            compiler_params=params(mib),
            cost_estimate=pl.CostEstimate(
                flops=int(work * flops), bytes_accessed=4 << 20, transcendentals=0
            ),
            name=name,
            **kw,
        )

    def low_pair(length):
        return [pltpu.VMEM((length * BLK, WIDE), BF16)] * 2

    grid = (KVH,)
    packed = pack(keys_in, values_in)
    slices = all_to_all(packed.reshape(count, rows, HD))
    inner, outer = swap_inner(packed), swap_outer(packed)
    slices, inner = lax.optimization_barrier((slices, inner))
    far = all_to_all(select(wanted, slices, heads))
    far, outer = lax.optimization_barrier((far, outer))
    if share == 1:
        far = far.reshape(2, KVH, BLK // rows, 2, rows, HD)
        far = jnp.transpose(far, (0, 1, 3, 2, 4, 5))
    far = far.reshape(2, KVH * share, 2, BLK // share, HD)
    other = mate(far)
    stats, glob, for_mate, random = call(
        scores_kernel,
        "scores",
        3,
        50,
        [smem, vmem, vmem] + [anywhere] * 5,
        [(vmem, jax.ShapeDtypeStruct((KVH, 8, WIDE), F32)), (vmem, wide)] + [(vmem, low)] * 2,
        [pltpu.VMEM((SLOTS * BLK, PART), F32)] * 2
        + low_pair(3)
        + [
            pltpu.VMEM((3, 2, KVH, BLK, HD), BF16),
            pltpu.VMEM((2, KVH, BLK, WIDE), BF16),
            pltpu.SemaphoreType.DMA((3,)),
            pltpu.SemaphoreType.DMA((2, KVH)),
        ],
    )(edges, far, other, queries, cotangent, inner, outer, packed)
    flat = (count, rows, HD)
    terms = join(random.reshape(flat), glob.reshape(flat), mate(for_mate).reshape(flat))
    arrived = all_to_all(terms)
    back = call(
        window_kernel, "window", 1, 56, [smem, token, token, block, block, stat],
        [(block, low)] * 2, low_pair(2), grid=grid,
    )(edges, queries, cotangent, inner, outer, stats)
    back = [swap_inner(back[0]), swap_outer(back[1])]
    arrived, *back = lax.optimization_barrier((arrived, *back))
    summed = combine(wanted, arrived, heads)
    returned = all_to_all(summed).reshape(2, KVH, BLK, HD)
    stats, summed = lax.optimization_barrier((stats, summed))
    attn_out, grad_query, near = call(
        outputs_kernel,
        "outputs",
        3,
        56,
        [smem, token, token] + [block] * 3 + [far_spec] * 2 + [stat, block, block],
        [(token, token_shape)] * 2 + [(block, wide)],
        low_pair(SLOTS),
        grid=grid,
    )(edges, queries, cotangent, packed, inner, outer, far, other, stats, *back)
    grad_keys, grad_values = finish(near, returned)
    return attn_out, grad_query, grad_keys, grad_values


def solution(mesh):
    spec = P(AXES, None)
    return jax.shard_map(
        shards,
        mesh=mesh,
        in_specs=(spec, spec, spec, spec, P(), P()),
        out_specs=(spec, spec, spec, spec),
        check_vma=False,
    )
```

```python
import math

import jax
import jax.numpy as jnp
from jax import lax
from jax.experimental import pallas as pl
from jax.experimental.pallas import tpu as pltpu
from jax.sharding import PartitionSpec as P

HD = 128
H = 32
KVH = 4
BLK = 128
NG = 2
GROUP = H // KVH
SCALE = 1.0 / math.sqrt(HD)
NEG_FILL = -1e30
AXES = ("ctx", "heads")
MATES = 2
SLOTS = 3 + NG + 1
WIDE = GROUP * BLK
PART = WIDE
PIECE = WIDE // 4
FACTOR = SCALE / math.log(2.0)
BF16 = jnp.bfloat16
F32 = jnp.float32

NT = (((1,), (1,)), ((), ()))


def params(mib, **kw):
    return pltpu.CompilerParams(vmem_limit_bytes=mib << 20, **kw)


def all_to_all(value):
    return lax.all_to_all(value, AXES, split_axis=0, concat_axis=0, tiled=True)


def mate(value):
    count = lax.axis_size("ctx")
    return lax.ppermute(value, "ctx", [(i, i ^ 1) for i in range(count)])


def swap_inner(value):
    heads = lax.axis_size("heads")
    return lax.ppermute(value, "heads", [(h, h ^ 1) for h in range(heads)])


def swap_outer(value):
    heads, ctx = lax.axis_size("heads"), lax.axis_size("ctx")
    pairs = []
    for i in range(1, heads * ctx - 1):
        j = i + 1 if i % 2 else i - 1
        pairs.append(tuple(b % heads * ctx + b // heads for b in (i, j)))
    return lax.ppermute(value, ("heads", "ctx"), pairs)


def pack_kernel(k_ref, v_ref, out_ref):
    for g in range(KVH):
        cols = slice(g * HD, (g + 1) * HD)
        out_ref[0, g] = k_ref[:, cols]
        out_ref[1, g] = v_ref[:, cols]


def pack(keys, values):
    return pl.pallas_call(
        pack_kernel,
        out_shape=jax.ShapeDtypeStruct((2, KVH, BLK, HD), BF16),
        compiler_params=params(58),
        name="pack",
    )(keys, values)


def side_of(i, heads):
    return i // heads % MATES


def select_kernel(heads, wanted_ref, in_ref, out_ref):
    count = in_ref.shape[0]
    globs = [in_ref[wanted_ref[count + slot]] for slot in range(NG)]
    for i in range(count):
        out_ref[i, 0] = in_ref[wanted_ref[i]]
        out_ref[i, 1] = globs[side_of(i, heads)]


def select(wanted, slices, heads):
    count, rows, _ = slices.shape
    if rows % 16:
        i = jnp.arange(count)
        glob = wanted[count + side_of(i, heads)]
        return slices[jnp.stack([wanted[i], glob], axis=1)]
    return pl.pallas_call(
        lambda *refs: select_kernel(heads, *refs),
        out_shape=jax.ShapeDtypeStruct((count, 2, rows, HD), BF16),
        in_specs=[
            pl.BlockSpec(memory_space=pltpu.SMEM),
            pl.BlockSpec(memory_space=pltpu.VMEM),
        ],
        out_specs=pl.BlockSpec(memory_space=pltpu.VMEM),
        compiler_params=params(8),
        name="select",
    )(wanted, slices)


def combine_kernel(heads, wanted_ref, in_ref, out_ref, acc_ref):
    count = in_ref.shape[0]
    acc_ref[...] = jnp.zeros_like(acc_ref)
    for side in range(MATES):
        total = None
        for i in range(count):
            if side_of(i, heads) == side:
                term = in_ref[i, 1].astype(F32)
                total = term if total is None else total + term
        acc_ref[wanted_ref[count + side]] += total
    for i in range(count):
        acc_ref[wanted_ref[i]] += in_ref[i, 0].astype(F32)
    out_ref[...] = acc_ref[...].astype(BF16)


def combine(wanted, terms, heads):
    count, _, rows, _ = terms.shape
    if rows % 16:
        i = jnp.arange(count)
        wide = terms.astype(F32)
        total = jnp.zeros((count, rows, HD), F32).at[wanted[i]].add(wide[:, 0])
        return total.at[wanted[count + side_of(i, heads)]].add(wide[:, 1]).astype(BF16)
    return pl.pallas_call(
        lambda *refs: combine_kernel(heads, *refs),
        out_shape=jax.ShapeDtypeStruct((count, rows, HD), BF16),
        in_specs=[
            pl.BlockSpec(memory_space=pltpu.SMEM),
            pl.BlockSpec(memory_space=pltpu.VMEM),
        ],
        out_specs=pl.BlockSpec(memory_space=pltpu.VMEM),
        scratch_shapes=[pltpu.VMEM((count, rows, HD), F32)],
        compiler_params=params(16),
        name="combine",
    )(wanted, terms)


def join_kernel(random_ref, glob_ref, other_ref, out_ref):
    out_ref[:, 0] = random_ref[...]
    out_ref[:, 1] = (glob_ref[...] + other_ref[...].astype(F32)).astype(BF16)


def join(random, glob, other):
    count, rows, _ = random.shape
    if rows % 16:
        total = (glob + other.astype(F32)).astype(BF16)
        return jnp.stack([random, total], axis=1)
    return pl.pallas_call(
        join_kernel,
        out_shape=jax.ShapeDtypeStruct((count, 2, rows, HD), BF16),
        compiler_params=params(8),
        name="join",
    )(random, glob, other)


def stacked(ref):
    return jnp.concatenate(
        [ref[:, h * HD : (h + 1) * HD] for h in range(GROUP)], axis=0
    )


def blocks_of(near, far_ref, other_ref):
    blocks = list(near)
    for ref, slot in ((far_ref, 1), (other_ref, 1), (far_ref, 0)):
        blocks.append(ref[:, slot].reshape(BLK, HD))
    return blocks


def dot_nt(a, b):
    return lax.dot_general(a, b, NT, preferred_element_type=F32)


def put_grads(rows, queries, douts, probs_ref, ds_ref, dests):
    dk = jnp.dot(ds_ref[rows], queries, preferred_element_type=F32) * SCALE
    dv = jnp.dot(probs_ref[rows], douts, preferred_element_type=F32)
    for i, dest in enumerate(dests):
        for kind, term in enumerate((dk, dv)):
            dest[kind] = term[i * BLK : (i + 1) * BLK].astype(dest.dtype)


def block_rows(b):
    return slice(b * BLK, (b + 1) * BLK)


def masked(edge_ref, b, scores):
    return jnp.where(edge_ref[0] == 0, scores, NEG_FILL) if b == 1 else scores


def first_kernel(q_ref, do_ref, own_ref, inner_ref, stats_ref):
    keys, values = (
        jnp.concatenate([own_ref[kind, 0], inner_ref[kind, 0]], axis=0)
        for kind in range(2)
    )
    queries, douts = stacked(q_ref), stacked(do_ref)
    for part in range(WIDE // PART):
        cols = slice(part * PART, (part + 1) * PART)
        s, dp = dot_nt(keys, queries[cols]), dot_nt(values, douts[cols])
        row_max = jnp.max(s, axis=0, keepdims=True)
        w = jnp.exp2((s - row_max) * FACTOR)
        stats_ref[0, 0:1, cols] = row_max
        stats_ref[0, 1:2, cols] = jnp.sum(w, axis=0, keepdims=True)
        stats_ref[0, 2:3, cols] = jnp.sum(w * dp, axis=0, keepdims=True)


def scores_kernel(
    edge_ref, far_ref, other_ref, first_ref, q_any, do_any, outer_any,
    stats_ref, glob_ref, mate_ref, random_ref,
    s_ref, dp_ref, probs_ref, ds_ref, outer_ref, tokens_ref, sem, token_sem,
):
    outer_copy = pltpu.make_async_copy(outer_any, outer_ref, sem)

    def token_copies(g):
        cols = pl.ds(pl.multiple_of(g * WIDE, WIDE), WIDE)
        return [
            pltpu.make_async_copy(
                ref.at[:, cols], tokens_ref.at[i, g], token_sem.at[i, g]
            )
            for i, ref in enumerate((q_any, do_any))
        ]

    outer_copy.start()
    for g in range(KVH):
        for copy in token_copies(g):
            copy.start()
    outer_copy.wait()
    share = far_ref.shape[1] // KVH
    count = SLOTS - 2

    def group(g, carry):
        for copy in token_copies(g):
            copy.wait()
        queries, douts = (stacked(tokens_ref.at[i, g]) for i in range(2))
        keys, values = (
            blocks_of(
                [outer_ref[kind, g]],
                far_ref.at[kind, pl.ds(g * share, share)],
                other_ref.at[kind, pl.ds(g * share, share)],
            )
            for kind in range(2)
        )
        for piece in range(WIDE // PIECE):
            cols = slice(piece * PIECE, (piece + 1) * PIECE)
            first_max = first_ref[g, 0:1, cols]
            row_max = first_max
            for b in range(count):
                score = dot_nt(keys[b], queries[cols])
                if b == 0:
                    score = jnp.where(edge_ref[0] == 0, score, NEG_FILL)
                s_ref[block_rows(b)] = score
                row_max = jnp.maximum(row_max, jnp.max(score, axis=0, keepdims=True))
            scale = jnp.exp2((first_max - row_max) * FACTOR)
            row_sum = first_ref[g, 1:2, cols] * scale
            centre = first_ref[g, 2:3, cols] * scale
            for b in range(count):
                w = jnp.exp2((s_ref[block_rows(b)] - row_max) * FACTOR)
                if b >= 1:
                    s_ref[block_rows(b)] = w
                dp = dot_nt(values[b], douts[cols])
                dp_ref[block_rows(b)] = dp
                row_sum = row_sum + jnp.sum(w, axis=0, keepdims=True)
                centre = centre + jnp.sum(w * dp, axis=0, keepdims=True)
            inverse = 1.0 / row_sum
            centre = centre * inverse
            stats_ref[g, 0:1, cols] = row_max
            stats_ref[g, 1:2, cols] = inverse
            stats_ref[g, 2:3, cols] = centre
            for b in range(1, count):
                rows = block_rows(b)
                p = s_ref[rows] * inverse
                dest = block_rows(b - 1)
                probs_ref[dest, cols] = p.astype(BF16)
                ds_ref[dest, cols] = (p * (dp_ref[rows] - centre)).astype(BF16)
        dests = [ref.at[:, g] for ref in (glob_ref, mate_ref, random_ref)]
        put_grads(slice(None), queries, douts, probs_ref, ds_ref, dests)
        return carry

    lax.fori_loop(0, KVH, group, 0)


def again(edge_ref, first, keys, values, q, do, stats_ref, probs_ref, ds_ref, cols):
    row_max, inverse, centre = (stats_ref[0, i : i + 1, cols] for i in range(3))
    s, dp = dot_nt(keys, q), dot_nt(values, do)
    for b in range(keys.shape[0] // BLK):
        rows = block_rows(b)
        score = masked(edge_ref, first + b, s[rows])
        p = jnp.exp2((score - row_max) * FACTOR) * inverse
        probs_ref[rows, cols] = p.astype(BF16)
        ds_ref[rows, cols] = (p * (dp[rows] - centre)).astype(BF16)


def window_kernel(
    edge_ref, q_ref, do_ref, inner_ref, outer_ref, stats_ref,
    to_inner_ref, to_outer_ref, probs_ref, ds_ref,
):
    keys, values = (
        jnp.concatenate([inner_ref[kind, 0], outer_ref[kind, 0]], axis=0)
        for kind in range(2)
    )
    queries, douts = stacked(q_ref), stacked(do_ref)
    for part in range(WIDE // PART):
        cols = slice(part * PART, (part + 1) * PART)
        again(
            edge_ref, 0, keys, values, queries[cols], douts[cols],
            stats_ref, probs_ref, ds_ref, cols,
        )
    put_grads(
        slice(None), queries, douts, probs_ref, ds_ref,
        (to_inner_ref.at[:, 0], to_outer_ref.at[:, 0]),
    )


def outputs_kernel(
    edge_ref, q_ref, do_ref, own_ref, inner_ref, outer_ref, far_ref, other_ref,
    stats_ref, from_inner_ref, from_outer_ref, out_ref, dq_ref, near_ref, probs_ref, ds_ref,
):
    key_blocks, value_blocks = (
        blocks_of(
            [ref[kind, 0] for ref in (inner_ref, outer_ref, own_ref)],
            far_ref.at[kind],
            other_ref.at[kind],
        )
        for kind in range(2)
    )
    keys, values = (jnp.concatenate(x, axis=0) for x in (key_blocks, value_blocks))
    keys_t, values_t = (
        jnp.concatenate([x.T for x in blocks], axis=1)
        for blocks in (key_blocks, value_blocks)
    )
    queries, douts = stacked(q_ref), stacked(do_ref)
    for part in range(WIDE // PART):
        cols = slice(part * PART, (part + 1) * PART)
        again(
            edge_ref, 0, keys, values, queries[cols], douts[cols],
            stats_ref, probs_ref, ds_ref, cols,
        )
        out_t = jnp.dot(values_t, probs_ref[:, cols], preferred_element_type=F32)
        dq_t = jnp.dot(keys_t, ds_ref[:, cols], preferred_element_type=F32) * SCALE
        for i in range(PART // HD):
            place = slice(i * HD, (i + 1) * HD)
            dest = slice(part * PART + i * HD, part * PART + (i + 1) * HD)
            out_ref[:, dest] = out_t[:, place].T.astype(BF16)
            dq_ref[:, dest] = dq_t[:, place].T.astype(BF16)
    put_grads(block_rows(2), queries, douts, probs_ref, ds_ref, (near_ref.at[:, 0],))
    for kind in range(2):
        back = from_inner_ref[kind, 0].astype(F32) + from_outer_ref[kind, 0].astype(F32)
        near_ref[kind, 0] += back


def finish_kernel(near_ref, far_ref, dk_ref, dv_ref):
    for kind, dest in enumerate((dk_ref, dv_ref)):
        for g in range(KVH):
            total = near_ref[kind, g] + far_ref[kind, g].astype(F32)
            dest[:, g * HD : (g + 1) * HD] = total.astype(BF16)


def finish(near, far):
    shape = jax.ShapeDtypeStruct((BLK, KVH * HD), BF16)
    return pl.pallas_call(
        finish_kernel,
        out_shape=(shape, shape),
        compiler_params=params(8),
        name="finish",
    )(near, far)


def shards(queries, keys_in, values_in, cotangent, rand_blocks, glob_blocks):
    heads, ctx = lax.axis_size("heads"), lax.axis_size("ctx")
    count = heads * ctx
    mine = lax.axis_index("ctx") * heads + lax.axis_index("heads")
    edges = ((mine == 0) | (mine == count - 1)).astype(jnp.int32).reshape(1)
    wanted = jnp.concatenate([rand_blocks[:, 0], glob_blocks])
    rows = 2 * KVH * BLK // count
    share = BLK // rows if rows % 16 == 0 else 1
    token = pl.BlockSpec((BLK, WIDE), lambda g: (0, g))
    block = pl.BlockSpec((2, 1, BLK, HD), lambda g: (0, g, 0, 0))
    far_spec = pl.BlockSpec((2, share, 2, BLK // share, HD), lambda g: (0, g, 0, 0, 0))
    stat = pl.BlockSpec((1, 8, WIDE), lambda g: (g, 0, 0))
    vmem = pl.BlockSpec(memory_space=pltpu.VMEM)
    smem = pl.BlockSpec(memory_space=pltpu.SMEM)
    anywhere = pl.BlockSpec(memory_space=pl.ANY)
    low, wide = (jax.ShapeDtypeStruct((2, KVH, BLK, HD), dtype) for dtype in (BF16, F32))
    stat_shape = jax.ShapeDtypeStruct((KVH, 8, WIDE), F32)
    token_shape = jax.ShapeDtypeStruct(queries.shape, BF16)
    flops = 2 * H * BLK * SLOTS * BLK * HD

    def call(kernel, name, work, mib, ins, outs, scratch=(), **kw):
        return pl.pallas_call(
            kernel,
            in_specs=ins,
            out_specs=[spec for spec, _ in outs],
            out_shape=[shape for _, shape in outs],
            scratch_shapes=scratch,
            compiler_params=params(mib),
            cost_estimate=pl.CostEstimate(
                flops=int(work * flops), bytes_accessed=4 << 20, transcendentals=0
            ),
            name=name,
            **kw,
        )

    def low_pair(length):
        return [pltpu.VMEM((length * BLK, WIDE), BF16)] * 2

    grid = (KVH,)
    packed = pack(keys_in, values_in)
    slices = all_to_all(packed.reshape(count, rows, HD))
    inner, outer = swap_inner(packed), swap_outer(packed)
    slices, inner = lax.optimization_barrier((slices, inner))
    far = all_to_all(select(wanted, slices, heads))
    first = call(
        first_kernel, "first", 1, 56, [token, token, block, block],
        [(stat, stat_shape)], grid=grid,
    )(queries, cotangent, packed, inner)[0]
    far, outer, first = lax.optimization_barrier((far, outer, first))
    if share == 1:
        far = far.reshape(2, KVH, BLK // rows, 2, rows, HD)
        far = jnp.transpose(far, (0, 1, 3, 2, 4, 5))
    far = far.reshape(2, KVH * share, 2, BLK // share, HD)
    other = mate(far)
    stats, glob, for_mate, random = call(
        scores_kernel,
        "scores",
        3,
        50,
        [smem, vmem, vmem, vmem] + [anywhere] * 3,
        [(vmem, stat_shape), (vmem, wide)] + [(vmem, low)] * 2,
        [pltpu.VMEM(((SLOTS - 2) * BLK, PIECE), F32)] * 2
        + low_pair(3)
        + [
            pltpu.VMEM((2, KVH, BLK, HD), BF16),
            pltpu.VMEM((2, KVH, BLK, WIDE), BF16),
            pltpu.SemaphoreType.DMA,
            pltpu.SemaphoreType.DMA((2, KVH)),
        ],
    )(edges, far, other, first, queries, cotangent, outer)
    flat = (count, rows, HD)
    terms = join(random.reshape(flat), glob.reshape(flat), mate(for_mate).reshape(flat))
    arrived = all_to_all(terms)
    back = call(
        window_kernel, "window", 1, 53, [smem, token, token, block, block, stat],
        [(block, low)] * 2, low_pair(2), grid=grid,
    )(edges, queries, cotangent, inner, outer, stats)
    back = [swap_inner(back[0]), swap_outer(back[1])]
    arrived, *back = lax.optimization_barrier((arrived, *back))
    summed = combine(wanted, arrived, heads)
    returned = all_to_all(summed).reshape(2, KVH, BLK, HD)
    stats, summed = lax.optimization_barrier((stats, summed))
    attn_out, grad_query, near = call(
        outputs_kernel,
        "outputs",
        3,
        53,
        [smem, token, token] + [block] * 3 + [far_spec] * 2 + [stat, block, block],
        [(token, token_shape)] * 2 + [(block, wide)],
        low_pair(SLOTS),
        grid=grid,
    )(edges, queries, cotangent, packed, inner, outer, far, other, stats, *back)
    grad_keys, grad_values = finish(near, returned)
    return attn_out, grad_query, grad_keys, grad_values


def solution(mesh):
    spec = P(AXES, None)
    return jax.shard_map(
        shards,
        mesh=mesh,
        in_specs=(spec, spec, spec, spec, P(), P()),
        out_specs=(spec, spec, spec, spec),
        check_vma=False,
    )
```

```python
import math

import jax
import jax.numpy as jnp
from jax import lax
from jax.experimental import pallas as pl
from jax.experimental.pallas import tpu as pltpu
from jax.sharding import PartitionSpec as P

HD = 128
H = 32
KVH = 4
BLK = 128
NG = 2
GROUP = H // KVH
SCALE = 1.0 / math.sqrt(HD)
NEG_FILL = -1e30
AXES = ("ctx", "heads")
MATES = 2
SLOTS = 3 + NG + 1
WIDE = GROUP * BLK
PART = WIDE
PIECE = WIDE // 4
FACTOR = SCALE / math.log(2.0)
BF16 = jnp.bfloat16
F32 = jnp.float32

NT = (((1,), (1,)), ((), ()))


def params(mib, **kw):
    return pltpu.CompilerParams(vmem_limit_bytes=mib << 20, **kw)


def all_to_all(value):
    return lax.all_to_all(value, AXES, split_axis=0, concat_axis=0, tiled=True)


def mate(value):
    count = lax.axis_size("ctx")
    return lax.ppermute(value, "ctx", [(i, i ^ 1) for i in range(count)])


def swap_inner(value):
    heads = lax.axis_size("heads")
    return lax.ppermute(value, "heads", [(h, h ^ 1) for h in range(heads)])


def swap_outer(value):
    heads, ctx = lax.axis_size("heads"), lax.axis_size("ctx")
    pairs = []
    for i in range(1, heads * ctx - 1):
        j = i + 1 if i % 2 else i - 1
        pairs.append(tuple(b % heads * ctx + b // heads for b in (i, j)))
    return lax.ppermute(value, ("heads", "ctx"), pairs)


def fetch_outer(own, inner):
    heads, ctx = lax.axis_size("heads"), lax.axis_size("ctx")
    count = heads * ctx
    pairs = []
    for i in range(count):
        step = 1 if i % 2 else -1
        j = i - 2 * step if i // heads % MATES else i + step
        if 0 <= j < count:
            pairs.append(tuple(b % heads * ctx + b // heads for b in (i, j)))
    value = jnp.where(lax.axis_index("ctx") % MATES == 0, own, inner)
    return lax.ppermute(value, ("heads", "ctx"), pairs)


def pack_kernel(k_ref, v_ref, out_ref):
    for g in range(KVH):
        cols = slice(g * HD, (g + 1) * HD)
        out_ref[0, g] = k_ref[:, cols]
        out_ref[1, g] = v_ref[:, cols]


def pack(keys, values):
    return pl.pallas_call(
        pack_kernel,
        out_shape=jax.ShapeDtypeStruct((2, KVH, BLK, HD), BF16),
        compiler_params=params(58),
        name="pack",
    )(keys, values)


def side_of(i, heads):
    return i // heads % MATES


def select_kernel(heads, wanted_ref, in_ref, out_ref):
    count = in_ref.shape[0]
    globs = [in_ref[wanted_ref[count + slot]] for slot in range(NG)]
    for i in range(count):
        out_ref[i, 0] = in_ref[wanted_ref[i]]
        out_ref[i, 1] = globs[side_of(i, heads)]


def select(wanted, slices, heads):
    count, rows, _ = slices.shape
    if rows % 16:
        i = jnp.arange(count)
        glob = wanted[count + side_of(i, heads)]
        return slices[jnp.stack([wanted[i], glob], axis=1)]
    return pl.pallas_call(
        lambda *refs: select_kernel(heads, *refs),
        out_shape=jax.ShapeDtypeStruct((count, 2, rows, HD), BF16),
        in_specs=[
            pl.BlockSpec(memory_space=pltpu.SMEM),
            pl.BlockSpec(memory_space=pltpu.VMEM),
        ],
        out_specs=pl.BlockSpec(memory_space=pltpu.VMEM),
        compiler_params=params(8),
        name="select",
    )(wanted, slices)


def combine_kernel(heads, wanted_ref, in_ref, out_ref, acc_ref):
    count = in_ref.shape[0]
    acc_ref[...] = jnp.zeros_like(acc_ref)
    for side in range(MATES):
        total = None
        for i in range(count):
            if side_of(i, heads) == side:
                term = in_ref[i, 1].astype(F32)
                total = term if total is None else total + term
        acc_ref[wanted_ref[count + side]] += total
    for i in range(count):
        acc_ref[wanted_ref[i]] += in_ref[i, 0].astype(F32)
    out_ref[...] = acc_ref[...].astype(BF16)


def combine(wanted, terms, heads):
    count, _, rows, _ = terms.shape
    if rows % 16:
        i = jnp.arange(count)
        wide = terms.astype(F32)
        total = jnp.zeros((count, rows, HD), F32).at[wanted[i]].add(wide[:, 0])
        return total.at[wanted[count + side_of(i, heads)]].add(wide[:, 1]).astype(BF16)
    return pl.pallas_call(
        lambda *refs: combine_kernel(heads, *refs),
        out_shape=jax.ShapeDtypeStruct((count, rows, HD), BF16),
        in_specs=[
            pl.BlockSpec(memory_space=pltpu.SMEM),
            pl.BlockSpec(memory_space=pltpu.VMEM),
        ],
        out_specs=pl.BlockSpec(memory_space=pltpu.VMEM),
        scratch_shapes=[pltpu.VMEM((count, rows, HD), F32)],
        compiler_params=params(16),
        name="combine",
    )(wanted, terms)


def join_kernel(random_ref, glob_ref, other_ref, out_ref):
    out_ref[:, 0] = random_ref[...]
    out_ref[:, 1] = (glob_ref[...] + other_ref[...].astype(F32)).astype(BF16)


def join(random, glob, other):
    count, rows, _ = random.shape
    if rows % 16:
        total = (glob + other.astype(F32)).astype(BF16)
        return jnp.stack([random, total], axis=1)
    return pl.pallas_call(
        join_kernel,
        out_shape=jax.ShapeDtypeStruct((count, 2, rows, HD), BF16),
        compiler_params=params(8),
        name="join",
    )(random, glob, other)


def stacked(ref):
    return jnp.concatenate(
        [ref[:, h * HD : (h + 1) * HD] for h in range(GROUP)], axis=0
    )


def blocks_of(near, far_ref, other_ref):
    blocks = list(near)
    for ref, slot in ((far_ref, 1), (other_ref, 1), (far_ref, 0)):
        blocks.append(ref[:, slot].reshape(BLK, HD))
    return blocks


def dot_nt(a, b):
    return lax.dot_general(a, b, NT, preferred_element_type=F32)


def put_grads(rows, queries, douts, probs_ref, ds_ref, dests):
    dk = jnp.dot(ds_ref[rows], queries, preferred_element_type=F32) * SCALE
    dv = jnp.dot(probs_ref[rows], douts, preferred_element_type=F32)
    for i, dest in enumerate(dests):
        for kind, term in enumerate((dk, dv)):
            dest[kind] = term[i * BLK : (i + 1) * BLK].astype(dest.dtype)


def block_rows(b):
    return slice(b * BLK, (b + 1) * BLK)


def masked(edge_ref, b, scores):
    return jnp.where(edge_ref[0] == 0, scores, NEG_FILL) if b == 1 else scores


def first_kernel(q_ref, do_ref, own_ref, inner_ref, stats_ref):
    keys, values = (
        jnp.concatenate([own_ref[kind, 0], inner_ref[kind, 0]], axis=0)
        for kind in range(2)
    )
    queries, douts = stacked(q_ref), stacked(do_ref)
    for part in range(WIDE // PART):
        cols = slice(part * PART, (part + 1) * PART)
        s, dp = dot_nt(keys, queries[cols]), dot_nt(values, douts[cols])
        row_max = jnp.max(s, axis=0, keepdims=True)
        w = jnp.exp2((s - row_max) * FACTOR)
        stats_ref[0, 0:1, cols] = row_max
        stats_ref[0, 1:2, cols] = jnp.sum(w, axis=0, keepdims=True)
        stats_ref[0, 2:3, cols] = jnp.sum(w * dp, axis=0, keepdims=True)


def scores_kernel(
    edge_ref, far_ref, other_ref, first_ref, q_any, do_any, outer_any,
    stats_ref, glob_ref, mate_ref, random_ref,
    s_ref, dp_ref, probs_ref, ds_ref, outer_ref, tokens_ref, sem, token_sem,
):
    outer_copy = pltpu.make_async_copy(outer_any, outer_ref, sem)

    def token_copies(g):
        cols = pl.ds(pl.multiple_of(g * WIDE, WIDE), WIDE)
        return [
            pltpu.make_async_copy(
                ref.at[:, cols], tokens_ref.at[i, g], token_sem.at[i, g]
            )
            for i, ref in enumerate((q_any, do_any))
        ]

    outer_copy.start()
    for g in range(KVH):
        for copy in token_copies(g):
            copy.start()
    outer_copy.wait()
    share = far_ref.shape[1] // KVH
    count = SLOTS - 2

    def group(g, carry):
        for copy in token_copies(g):
            copy.wait()
        queries, douts = (stacked(tokens_ref.at[i, g]) for i in range(2))
        keys, values = (
            blocks_of(
                [outer_ref[kind, g]],
                far_ref.at[kind, pl.ds(g * share, share)],
                other_ref.at[kind, pl.ds(g * share, share)],
            )
            for kind in range(2)
        )
        for piece in range(WIDE // PIECE):
            cols = slice(piece * PIECE, (piece + 1) * PIECE)
            first_max = first_ref[g, 0:1, cols]
            row_max = first_max
            for b in range(count):
                score = dot_nt(keys[b], queries[cols])
                if b == 0:
                    score = jnp.where(edge_ref[0] == 0, score, NEG_FILL)
                s_ref[block_rows(b)] = score
                row_max = jnp.maximum(row_max, jnp.max(score, axis=0, keepdims=True))
            scale = jnp.exp2((first_max - row_max) * FACTOR)
            row_sum = first_ref[g, 1:2, cols] * scale
            centre = first_ref[g, 2:3, cols] * scale
            for b in range(count):
                w = jnp.exp2((s_ref[block_rows(b)] - row_max) * FACTOR)
                if b >= 1:
                    s_ref[block_rows(b)] = w
                dp = dot_nt(values[b], douts[cols])
                dp_ref[block_rows(b)] = dp
                row_sum = row_sum + jnp.sum(w, axis=0, keepdims=True)
                centre = centre + jnp.sum(w * dp, axis=0, keepdims=True)
            inverse = 1.0 / row_sum
            centre = centre * inverse
            stats_ref[g, 0:1, cols] = row_max
            stats_ref[g, 1:2, cols] = inverse
            stats_ref[g, 2:3, cols] = centre
            for b in range(1, count):
                rows = block_rows(b)
                p = s_ref[rows] * inverse
                dest = block_rows(b - 1)
                probs_ref[dest, cols] = p.astype(BF16)
                ds_ref[dest, cols] = (p * (dp_ref[rows] - centre)).astype(BF16)
        dests = [ref.at[:, g] for ref in (glob_ref, mate_ref, random_ref)]
        put_grads(slice(None), queries, douts, probs_ref, ds_ref, dests)
        return carry

    lax.fori_loop(0, KVH, group, 0)


def again(edge_ref, first, keys, values, q, do, stats_ref, probs_ref, ds_ref, cols):
    row_max, inverse, centre = (stats_ref[0, i : i + 1, cols] for i in range(3))
    s, dp = dot_nt(keys, q), dot_nt(values, do)
    for b in range(keys.shape[0] // BLK):
        rows = block_rows(b)
        score = masked(edge_ref, first + b, s[rows])
        p = jnp.exp2((score - row_max) * FACTOR) * inverse
        probs_ref[rows, cols] = p.astype(BF16)
        ds_ref[rows, cols] = (p * (dp[rows] - centre)).astype(BF16)


def window_kernel(
    edge_ref, q_ref, do_ref, inner_ref, outer_ref, stats_ref,
    to_inner_ref, to_outer_ref, probs_ref, ds_ref,
):
    keys, values = (
        jnp.concatenate([inner_ref[kind, 0], outer_ref[kind, 0]], axis=0)
        for kind in range(2)
    )
    queries, douts = stacked(q_ref), stacked(do_ref)
    for part in range(WIDE // PART):
        cols = slice(part * PART, (part + 1) * PART)
        again(
            edge_ref, 0, keys, values, queries[cols], douts[cols],
            stats_ref, probs_ref, ds_ref, cols,
        )
    put_grads(
        slice(None), queries, douts, probs_ref, ds_ref,
        (to_inner_ref.at[:, 0], to_outer_ref.at[:, 0]),
    )


def outputs_kernel(
    edge_ref, q_ref, do_ref, own_ref, inner_ref, outer_ref, far_ref, other_ref,
    stats_ref, from_inner_ref, from_outer_ref, out_ref, dq_ref, near_ref, probs_ref, ds_ref,
):
    key_blocks, value_blocks = (
        blocks_of(
            [ref[kind, 0] for ref in (inner_ref, outer_ref, own_ref)],
            far_ref.at[kind],
            other_ref.at[kind],
        )
        for kind in range(2)
    )
    keys, values = (jnp.concatenate(x, axis=0) for x in (key_blocks, value_blocks))
    keys_t, values_t = (
        jnp.concatenate([x.T for x in blocks], axis=1)
        for blocks in (key_blocks, value_blocks)
    )
    queries, douts = stacked(q_ref), stacked(do_ref)
    for part in range(WIDE // PART):
        cols = slice(part * PART, (part + 1) * PART)
        again(
            edge_ref, 0, keys, values, queries[cols], douts[cols],
            stats_ref, probs_ref, ds_ref, cols,
        )
        out_t = jnp.dot(values_t, probs_ref[:, cols], preferred_element_type=F32)
        dq_t = jnp.dot(keys_t, ds_ref[:, cols], preferred_element_type=F32) * SCALE
        for i in range(PART // HD):
            place = slice(i * HD, (i + 1) * HD)
            dest = slice(part * PART + i * HD, part * PART + (i + 1) * HD)
            out_ref[:, dest] = out_t[:, place].T.astype(BF16)
            dq_ref[:, dest] = dq_t[:, place].T.astype(BF16)
    put_grads(block_rows(2), queries, douts, probs_ref, ds_ref, (near_ref.at[:, 0],))
    for kind in range(2):
        back = from_inner_ref[kind, 0].astype(F32) + from_outer_ref[kind, 0].astype(F32)
        near_ref[kind, 0] += back


def finish_kernel(near_ref, far_ref, dk_ref, dv_ref):
    for kind, dest in enumerate((dk_ref, dv_ref)):
        for g in range(KVH):
            total = near_ref[kind, g] + far_ref[kind, g].astype(F32)
            dest[:, g * HD : (g + 1) * HD] = total.astype(BF16)


def finish(near, far):
    shape = jax.ShapeDtypeStruct((BLK, KVH * HD), BF16)
    return pl.pallas_call(
        finish_kernel,
        out_shape=(shape, shape),
        compiler_params=params(8),
        name="finish",
    )(near, far)


def shards(queries, keys_in, values_in, cotangent, rand_blocks, glob_blocks):
    heads, ctx = lax.axis_size("heads"), lax.axis_size("ctx")
    count = heads * ctx
    mine = lax.axis_index("ctx") * heads + lax.axis_index("heads")
    edges = ((mine == 0) | (mine == count - 1)).astype(jnp.int32).reshape(1)
    wanted = jnp.concatenate([rand_blocks[:, 0], glob_blocks])
    rows = 2 * KVH * BLK // count
    share = BLK // rows if rows % 16 == 0 else 1
    token = pl.BlockSpec((BLK, WIDE), lambda g: (0, g))
    block = pl.BlockSpec((2, 1, BLK, HD), lambda g: (0, g, 0, 0))
    far_spec = pl.BlockSpec((2, share, 2, BLK // share, HD), lambda g: (0, g, 0, 0, 0))
    stat = pl.BlockSpec((1, 8, WIDE), lambda g: (g, 0, 0))
    vmem = pl.BlockSpec(memory_space=pltpu.VMEM)
    smem = pl.BlockSpec(memory_space=pltpu.SMEM)
    anywhere = pl.BlockSpec(memory_space=pl.ANY)
    low, wide = (jax.ShapeDtypeStruct((2, KVH, BLK, HD), dtype) for dtype in (BF16, F32))
    stat_shape = jax.ShapeDtypeStruct((KVH, 8, WIDE), F32)
    token_shape = jax.ShapeDtypeStruct(queries.shape, BF16)
    flops = 2 * H * BLK * SLOTS * BLK * HD

    def call(kernel, name, work, mib, ins, outs, scratch=(), **kw):
        return pl.pallas_call(
            kernel,
            in_specs=ins,
            out_specs=[spec for spec, _ in outs],
            out_shape=[shape for _, shape in outs],
            scratch_shapes=scratch,
            compiler_params=params(mib),
            cost_estimate=pl.CostEstimate(
                flops=int(work * flops), bytes_accessed=4 << 20, transcendentals=0
            ),
            name=name,
            **kw,
        )

    def low_pair(length):
        return [pltpu.VMEM((length * BLK, WIDE), BF16)] * 2

    grid = (KVH,)
    packed = pack(keys_in, values_in)
    slices = all_to_all(packed.reshape(count, rows, HD))
    inner = swap_inner(packed)
    slices, inner = lax.optimization_barrier((slices, inner))
    outer = fetch_outer(packed, inner)
    far = all_to_all(select(wanted, slices, heads))
    first = call(
        first_kernel, "first", 1, 53, [token, token, block, block],
        [(stat, stat_shape)], grid=grid,
    )(queries, cotangent, packed, inner)[0]
    far, outer, first = lax.optimization_barrier((far, outer, first))
    if share == 1:
        far = far.reshape(2, KVH, BLK // rows, 2, rows, HD)
        far = jnp.transpose(far, (0, 1, 3, 2, 4, 5))
    far = far.reshape(2, KVH * share, 2, BLK // share, HD)
    other = mate(far)
    stats, glob, for_mate, random = call(
        scores_kernel,
        "scores",
        3,
        50,
        [smem, vmem, vmem, vmem] + [anywhere] * 3,
        [(vmem, stat_shape), (vmem, wide)] + [(vmem, low)] * 2,
        [pltpu.VMEM(((SLOTS - 2) * BLK, PIECE), F32)] * 2
        + low_pair(3)
        + [
            pltpu.VMEM((2, KVH, BLK, HD), BF16),
            pltpu.VMEM((2, KVH, BLK, WIDE), BF16),
            pltpu.SemaphoreType.DMA,
            pltpu.SemaphoreType.DMA((2, KVH)),
        ],
    )(edges, far, other, first, queries, cotangent, outer)
    flat = (count, rows, HD)
    terms = join(random.reshape(flat), glob.reshape(flat), mate(for_mate).reshape(flat))
    arrived = all_to_all(terms)
    back = call(
        window_kernel, "window", 1, 53, [smem, token, token, block, block, stat],
        [(block, low)] * 2, low_pair(2), grid=grid,
    )(edges, queries, cotangent, inner, outer, stats)
    back = [swap_inner(back[0]), swap_outer(back[1])]
    arrived, *back = lax.optimization_barrier((arrived, *back))
    summed = combine(wanted, arrived, heads)
    returned = all_to_all(summed).reshape(2, KVH, BLK, HD)
    stats, summed = lax.optimization_barrier((stats, summed))
    attn_out, grad_query, near = call(
        outputs_kernel,
        "outputs",
        3,
        53,
        [smem, token, token] + [block] * 3 + [far_spec] * 2 + [stat, block, block],
        [(token, token_shape)] * 2 + [(block, wide)],
        low_pair(SLOTS),
        grid=grid,
    )(edges, queries, cotangent, packed, inner, outer, far, other, stats, *back)
    grad_keys, grad_values = finish(near, returned)
    return attn_out, grad_query, grad_keys, grad_values


def solution(mesh):
    spec = P(AXES, None)
    return jax.shard_map(
        shards,
        mesh=mesh,
        in_specs=(spec, spec, spec, spec, P(), P()),
        out_specs=(spec, spec, spec, spec),
        check_vma=False,
    )
```

```python
import math

import jax
import jax.numpy as jnp
from jax import lax
from jax.experimental import pallas as pl
from jax.experimental.pallas import tpu as pltpu
from jax.sharding import PartitionSpec as P

HD = 128
H = 32
KVH = 4
BLK = 128
NG = 2
GROUP = H // KVH
SCALE = 1.0 / math.sqrt(HD)
NEG_FILL = -1e30
AXES = ("ctx", "heads")
MATES = 2
SLOTS = 3 + NG + 1
WIDE = GROUP * BLK
PART = WIDE
PIECE = WIDE // 4
FACTOR = SCALE / math.log(2.0)
BF16 = jnp.bfloat16
F32 = jnp.float32

NT = (((1,), (1,)), ((), ()))


def params(mib, **kw):
    return pltpu.CompilerParams(vmem_limit_bytes=mib << 20, **kw)


def all_to_all(value):
    return lax.all_to_all(value, AXES, split_axis=0, concat_axis=0, tiled=True)


def mate(value):
    count = lax.axis_size("ctx")
    return lax.ppermute(value, "ctx", [(i, i ^ 1) for i in range(count)])


def swap_inner(value):
    heads = lax.axis_size("heads")
    return lax.ppermute(value, "heads", [(h, h ^ 1) for h in range(heads)])


def swap_outer(value):
    heads, ctx = lax.axis_size("heads"), lax.axis_size("ctx")
    pairs = []
    for i in range(1, heads * ctx - 1):
        j = i + 1 if i % 2 else i - 1
        pairs.append(tuple(b % heads * ctx + b // heads for b in (i, j)))
    return lax.ppermute(value, ("heads", "ctx"), pairs)


def fetch_outer(own, inner):
    heads, ctx = lax.axis_size("heads"), lax.axis_size("ctx")
    count = heads * ctx
    pairs = []
    for i in range(count):
        step = 1 if i % 2 else -1
        j = i - 2 * step if i // heads % MATES else i + step
        if 0 <= j < count:
            pairs.append(tuple(b % heads * ctx + b // heads for b in (i, j)))
    value = jnp.where(lax.axis_index("ctx") % MATES == 0, own, inner)
    return lax.ppermute(value, ("heads", "ctx"), pairs)


def pack_kernel(k_ref, v_ref, out_ref):
    for g in range(KVH):
        cols = slice(g * HD, (g + 1) * HD)
        out_ref[0, g] = k_ref[:, cols]
        out_ref[1, g] = v_ref[:, cols]


def pack(keys, values):
    return pl.pallas_call(
        pack_kernel,
        out_shape=jax.ShapeDtypeStruct((2, KVH, BLK, HD), BF16),
        compiler_params=params(58),
        name="pack",
    )(keys, values)


def side_of(i, heads):
    return i // heads % MATES


def select_kernel(heads, wanted_ref, in_ref, out_ref):
    count = in_ref.shape[0]
    globs = [in_ref[wanted_ref[count + slot]] for slot in range(NG)]
    for i in range(count):
        out_ref[i, 0] = in_ref[wanted_ref[i]]
        out_ref[i, 1] = globs[side_of(i, heads)]


def select(wanted, slices, heads):
    count, rows, _ = slices.shape
    if rows % 16:
        i = jnp.arange(count)
        glob = wanted[count + side_of(i, heads)]
        return slices[jnp.stack([wanted[i], glob], axis=1)]
    return pl.pallas_call(
        lambda *refs: select_kernel(heads, *refs),
        out_shape=jax.ShapeDtypeStruct((count, 2, rows, HD), BF16),
        in_specs=[
            pl.BlockSpec(memory_space=pltpu.SMEM),
            pl.BlockSpec(memory_space=pltpu.VMEM),
        ],
        out_specs=pl.BlockSpec(memory_space=pltpu.VMEM),
        compiler_params=params(8),
        name="select",
    )(wanted, slices)


def combine_kernel(heads, wanted_ref, in_ref, out_ref, acc_ref):
    count = in_ref.shape[0]
    acc_ref[...] = jnp.zeros_like(acc_ref)
    for side in range(MATES):
        total = None
        for i in range(count):
            if side_of(i, heads) == side:
                term = in_ref[i, 1].astype(F32)
                total = term if total is None else total + term
        acc_ref[wanted_ref[count + side]] += total
    for i in range(count):
        acc_ref[wanted_ref[i]] += in_ref[i, 0].astype(F32)
    out_ref[...] = acc_ref[...].astype(BF16)


def combine(wanted, terms, heads):
    count, _, rows, _ = terms.shape
    if rows % 16:
        i = jnp.arange(count)
        wide = terms.astype(F32)
        total = jnp.zeros((count, rows, HD), F32).at[wanted[i]].add(wide[:, 0])
        return total.at[wanted[count + side_of(i, heads)]].add(wide[:, 1]).astype(BF16)
    return pl.pallas_call(
        lambda *refs: combine_kernel(heads, *refs),
        out_shape=jax.ShapeDtypeStruct((count, rows, HD), BF16),
        in_specs=[
            pl.BlockSpec(memory_space=pltpu.SMEM),
            pl.BlockSpec(memory_space=pltpu.VMEM),
        ],
        out_specs=pl.BlockSpec(memory_space=pltpu.VMEM),
        scratch_shapes=[pltpu.VMEM((count, rows, HD), F32)],
        compiler_params=params(16),
        name="combine",
    )(wanted, terms)


def join_kernel(random_ref, glob_ref, other_ref, out_ref):
    out_ref[:, 0] = random_ref[...]
    out_ref[:, 1] = (glob_ref[...] + other_ref[...].astype(F32)).astype(BF16)


def join(random, glob, other):
    count, rows, _ = random.shape
    if rows % 16:
        total = (glob + other.astype(F32)).astype(BF16)
        return jnp.stack([random, total], axis=1)
    return pl.pallas_call(
        join_kernel,
        out_shape=jax.ShapeDtypeStruct((count, 2, rows, HD), BF16),
        compiler_params=params(8),
        name="join",
    )(random, glob, other)


def stacked(ref):
    return jnp.concatenate(
        [ref[:, h * HD : (h + 1) * HD] for h in range(GROUP)], axis=0
    )


def blocks_of(near, far_ref, other_ref):
    blocks = list(near)
    for ref, slot in ((far_ref, 1), (other_ref, 1), (far_ref, 0)):
        blocks.append(ref[:, slot].reshape(BLK, HD))
    return blocks


def dot_nt(a, b):
    return lax.dot_general(a, b, NT, preferred_element_type=F32)


def put_grads(rows, queries, douts, probs_ref, ds_ref, dests):
    dk = jnp.dot(ds_ref[rows], queries, preferred_element_type=F32) * SCALE
    dv = jnp.dot(probs_ref[rows], douts, preferred_element_type=F32)
    for i, dest in enumerate(dests):
        for kind, term in enumerate((dk, dv)):
            dest[kind] = term[i * BLK : (i + 1) * BLK].astype(dest.dtype)


def block_rows(b):
    return slice(b * BLK, (b + 1) * BLK)


def masked(edge_ref, b, scores):
    return jnp.where(edge_ref[0] == 0, scores, NEG_FILL) if b == 1 else scores


def first_kernel(q_ref, do_ref, own_ref, inner_ref, stats_ref):
    keys, values = (
        jnp.concatenate([own_ref[kind, 0], inner_ref[kind, 0]], axis=0)
        for kind in range(2)
    )
    queries, douts = stacked(q_ref), stacked(do_ref)
    for part in range(WIDE // PART):
        cols = slice(part * PART, (part + 1) * PART)
        s, dp = dot_nt(keys, queries[cols]), dot_nt(values, douts[cols])
        row_max = jnp.max(s, axis=0, keepdims=True)
        w = jnp.exp2((s - row_max) * FACTOR)
        stats_ref[0, 0:1, cols] = row_max
        stats_ref[0, 1:2, cols] = jnp.sum(w, axis=0, keepdims=True)
        stats_ref[0, 2:3, cols] = jnp.sum(w * dp, axis=0, keepdims=True)


def scores_kernel(
    edge_ref, far_ref, other_ref, first_ref, q_any, do_any, outer_any,
    stats_ref, glob_ref, mate_ref, random_ref,
    s_ref, dp_ref, probs_ref, ds_ref, outer_ref, tokens_ref, sem, token_sem,
):
    outer_copy = pltpu.make_async_copy(outer_any, outer_ref, sem)

    def token_copies(g):
        cols = pl.ds(pl.multiple_of(g * WIDE, WIDE), WIDE)
        return [
            pltpu.make_async_copy(
                ref.at[:, cols], tokens_ref.at[i, g], token_sem.at[i, g]
            )
            for i, ref in enumerate((q_any, do_any))
        ]

    outer_copy.start()
    for g in range(KVH):
        for copy in token_copies(g):
            copy.start()
    outer_copy.wait()
    share = far_ref.shape[1] // KVH
    count = SLOTS - 2

    def group(g, carry):
        for copy in token_copies(g):
            copy.wait()
        queries, douts = (stacked(tokens_ref.at[i, g]) for i in range(2))
        keys, values = (
            blocks_of(
                [outer_ref[kind, g]],
                far_ref.at[kind, pl.ds(g * share, share)],
                other_ref.at[kind, pl.ds(g * share, share)],
            )
            for kind in range(2)
        )
        for piece in range(WIDE // PIECE):
            cols = slice(piece * PIECE, (piece + 1) * PIECE)
            first_max = first_ref[g, 0:1, cols]
            row_max = first_max
            for b in range(count):
                score = dot_nt(keys[b], queries[cols])
                if b == 0:
                    score = jnp.where(edge_ref[0] == 0, score, NEG_FILL)
                s_ref[block_rows(b)] = score
                row_max = jnp.maximum(row_max, jnp.max(score, axis=0, keepdims=True))
            scale = jnp.exp2((first_max - row_max) * FACTOR)
            row_sum = first_ref[g, 1:2, cols] * scale
            centre = first_ref[g, 2:3, cols] * scale
            for b in range(count):
                w = jnp.exp2((s_ref[block_rows(b)] - row_max) * FACTOR)
                if b >= 1:
                    s_ref[block_rows(b)] = w
                dp = dot_nt(values[b], douts[cols])
                dp_ref[block_rows(b)] = dp
                row_sum = row_sum + jnp.sum(w, axis=0, keepdims=True)
                centre = centre + jnp.sum(w * dp, axis=0, keepdims=True)
            inverse = 1.0 / row_sum
            centre = centre * inverse
            stats_ref[g, 0:1, cols] = row_max
            stats_ref[g, 1:2, cols] = inverse
            stats_ref[g, 2:3, cols] = centre
            for b in range(1, count):
                rows = block_rows(b)
                p = s_ref[rows] * inverse
                dest = block_rows(b - 1)
                probs_ref[dest, cols] = p.astype(BF16)
                ds_ref[dest, cols] = (p * (dp_ref[rows] - centre)).astype(BF16)
        dests = [ref.at[:, g] for ref in (glob_ref, mate_ref, random_ref)]
        put_grads(slice(None), queries, douts, probs_ref, ds_ref, dests)
        return carry

    lax.fori_loop(0, KVH, group, 0)


def again(edge_ref, first, keys, values, q, do, stats_ref, probs_ref, ds_ref, cols):
    row_max, inverse, centre = (stats_ref[0, i : i + 1, cols] for i in range(3))
    s, dp = dot_nt(keys, q), dot_nt(values, do)
    for b in range(keys.shape[0] // BLK):
        rows = block_rows(b)
        score = masked(edge_ref, first + b, s[rows])
        p = jnp.exp2((score - row_max) * FACTOR) * inverse
        probs_ref[rows, cols] = p.astype(BF16)
        ds_ref[rows, cols] = (p * (dp[rows] - centre)).astype(BF16)


def window_kernel(
    edge_ref, q_ref, do_ref, inner_ref, outer_ref, stats_ref,
    to_inner_ref, to_outer_ref, probs_ref, ds_ref,
):
    keys, values = (
        jnp.concatenate([inner_ref[kind, 0], outer_ref[kind, 0]], axis=0)
        for kind in range(2)
    )
    queries, douts = stacked(q_ref), stacked(do_ref)
    for part in range(WIDE // PART):
        cols = slice(part * PART, (part + 1) * PART)
        again(
            edge_ref, 0, keys, values, queries[cols], douts[cols],
            stats_ref, probs_ref, ds_ref, cols,
        )
    put_grads(
        slice(None), queries, douts, probs_ref, ds_ref,
        (to_inner_ref.at[:, 0], to_outer_ref.at[:, 0]),
    )


def outputs_kernel(
    edge_ref, q_ref, do_ref, own_ref, inner_ref, outer_ref, far_ref, other_ref,
    stats_ref, from_inner_ref, from_outer_ref, out_ref, dq_ref, near_ref, probs_ref, ds_ref,
):
    key_blocks, value_blocks = (
        blocks_of(
            [ref[kind, 0] for ref in (inner_ref, outer_ref, own_ref)],
            far_ref.at[kind],
            other_ref.at[kind],
        )
        for kind in range(2)
    )
    keys, values = (jnp.concatenate(x, axis=0) for x in (key_blocks, value_blocks))
    keys_t, values_t = (
        jnp.concatenate([x.T for x in blocks], axis=1)
        for blocks in (key_blocks, value_blocks)
    )
    queries, douts = stacked(q_ref), stacked(do_ref)
    for part in range(WIDE // PART):
        cols = slice(part * PART, (part + 1) * PART)
        again(
            edge_ref, 0, keys, values, queries[cols], douts[cols],
            stats_ref, probs_ref, ds_ref, cols,
        )
        out_t = jnp.dot(values_t, probs_ref[:, cols], preferred_element_type=F32)
        dq_t = jnp.dot(keys_t, ds_ref[:, cols], preferred_element_type=F32) * SCALE
        for i in range(PART // HD):
            place = slice(i * HD, (i + 1) * HD)
            dest = slice(part * PART + i * HD, part * PART + (i + 1) * HD)
            out_ref[:, dest] = out_t[:, place].T.astype(BF16)
            dq_ref[:, dest] = dq_t[:, place].T.astype(BF16)
    put_grads(block_rows(2), queries, douts, probs_ref, ds_ref, (near_ref.at[:, 0],))
    for kind in range(2):
        back = from_inner_ref[kind, 0].astype(F32) + from_outer_ref[kind, 0].astype(F32)
        near_ref[kind, 0] += back


def finish_kernel(near_ref, far_ref, dk_ref, dv_ref):
    for kind, dest in enumerate((dk_ref, dv_ref)):
        for g in range(KVH):
            total = near_ref[kind, g] + far_ref[kind, g].astype(F32)
            dest[:, g * HD : (g + 1) * HD] = total.astype(BF16)


def finish(near, far):
    shape = jax.ShapeDtypeStruct((BLK, KVH * HD), BF16)
    return pl.pallas_call(
        finish_kernel,
        out_shape=(shape, shape),
        compiler_params=params(8),
        name="finish",
    )(near, far)


def shards(queries, keys_in, values_in, cotangent, rand_blocks, glob_blocks):
    heads, ctx = lax.axis_size("heads"), lax.axis_size("ctx")
    count = heads * ctx
    mine = lax.axis_index("ctx") * heads + lax.axis_index("heads")
    edges = ((mine == 0) | (mine == count - 1)).astype(jnp.int32).reshape(1)
    wanted = jnp.concatenate([rand_blocks[:, 0], glob_blocks])
    rows = 2 * KVH * BLK // count
    share = BLK // rows if rows % 16 == 0 else 1
    token = pl.BlockSpec((BLK, WIDE), lambda g: (0, g))
    block = pl.BlockSpec((2, 1, BLK, HD), lambda g: (0, g, 0, 0))
    far_spec = pl.BlockSpec((2, share, 2, BLK // share, HD), lambda g: (0, g, 0, 0, 0))
    stat = pl.BlockSpec((1, 8, WIDE), lambda g: (g, 0, 0))
    vmem = pl.BlockSpec(memory_space=pltpu.VMEM)
    smem = pl.BlockSpec(memory_space=pltpu.SMEM)
    anywhere = pl.BlockSpec(memory_space=pl.ANY)
    low, wide = (jax.ShapeDtypeStruct((2, KVH, BLK, HD), dtype) for dtype in (BF16, F32))
    stat_shape = jax.ShapeDtypeStruct((KVH, 8, WIDE), F32)
    token_shape = jax.ShapeDtypeStruct(queries.shape, BF16)
    flops = 2 * H * BLK * SLOTS * BLK * HD

    def call(kernel, name, work, mib, ins, outs, scratch=(), **kw):
        return pl.pallas_call(
            kernel,
            in_specs=ins,
            out_specs=[spec for spec, _ in outs],
            out_shape=[shape for _, shape in outs],
            scratch_shapes=scratch,
            compiler_params=params(mib),
            cost_estimate=pl.CostEstimate(
                flops=int(work * flops), bytes_accessed=4 << 20, transcendentals=0
            ),
            name=name,
            **kw,
        )

    def low_pair(length):
        return [pltpu.VMEM((length * BLK, WIDE), BF16)] * 2

    grid = (KVH,)
    packed = pack(keys_in, values_in)
    slices = all_to_all(packed.reshape(count, rows, HD))
    inner = swap_inner(packed)
    slices, inner = lax.optimization_barrier((slices, inner))
    outer = fetch_outer(packed, inner)
    far = all_to_all(select(wanted, slices, heads))
    first = call(
        first_kernel, "first", 1, 53, [token, token, block, block],
        [(stat, stat_shape)], grid=grid,
    )(queries, cotangent, packed, inner)[0]
    far, outer, first = lax.optimization_barrier((far, outer, first))
    if share == 1:
        far = far.reshape(2, KVH, BLK // rows, 2, rows, HD)
        far = jnp.transpose(far, (0, 1, 3, 2, 4, 5))
    far = far.reshape(2, KVH * share, 2, BLK // share, HD)
    other = mate(far)
    stats, glob, for_mate, random = call(
        scores_kernel,
        "scores",
        3,
        50,
        [smem, vmem, vmem, vmem] + [anywhere] * 3,
        [(vmem, stat_shape), (vmem, wide)] + [(vmem, low)] * 2,
        [pltpu.VMEM(((SLOTS - 2) * BLK, PIECE), F32)] * 2
        + low_pair(3)
        + [
            pltpu.VMEM((2, KVH, BLK, HD), BF16),
            pltpu.VMEM((2, KVH, BLK, WIDE), BF16),
            pltpu.SemaphoreType.DMA,
            pltpu.SemaphoreType.DMA((2, KVH)),
        ],
    )(edges, far, other, first, queries, cotangent, outer)
    flat = (count, rows, HD)
    terms = join(random.reshape(flat), glob.reshape(flat), mate(for_mate).reshape(flat))
    arrived = all_to_all(terms)
    back = call(
        window_kernel, "window", 1, 53, [smem, token, token, block, block, stat],
        [(block, low)] * 2, low_pair(2), grid=grid,
    )(edges, queries, cotangent, inner, outer, stats)
    back = [swap_inner(back[0]), swap_outer(back[1])]
    arrived, *back = lax.optimization_barrier((arrived, *back))
    summed = combine(wanted, arrived, heads)
    returned = all_to_all(summed).reshape(2, KVH, BLK, HD)
    stats, summed = lax.optimization_barrier((stats, summed))
    attn_out, grad_query, near = call(
        outputs_kernel,
        "outputs",
        3,
        52,
        [smem, token, token] + [block] * 3 + [far_spec] * 2 + [stat, block, block],
        [(token, token_shape)] * 2 + [(block, wide)],
        low_pair(SLOTS),
        grid=grid,
    )(edges, queries, cotangent, packed, inner, outer, far, other, stats, *back)
    grad_keys, grad_values = finish(near, returned)
    return attn_out, grad_query, grad_keys, grad_values


def solution(mesh):
    spec = P(AXES, None)
    return jax.shard_map(
        shards,
        mesh=mesh,
        in_specs=(spec, spec, spec, spec, P(), P()),
        out_specs=(spec, spec, spec, spec),
        check_vma=False,
    )
```

```python
import math

import jax
import jax.numpy as jnp
from jax import lax
from jax.experimental import pallas as pl
from jax.experimental.pallas import tpu as pltpu
from jax.sharding import PartitionSpec as P

HD = 128
H = 32
KVH = 4
BLK = 128
NG = 2
GROUP = H // KVH
SCALE = 1.0 / math.sqrt(HD)
NEG_FILL = -1e30
AXES = ("ctx", "heads")
MATES = 2
SLOTS = 3 + NG + 1
WIDE = GROUP * BLK
PART = WIDE // 2
PIECE = WIDE // 4
FACTOR = SCALE / math.log(2.0)
BF16 = jnp.bfloat16
F32 = jnp.float32

NT = (((1,), (1,)), ((), ()))


def params(mib, **kw):
    return pltpu.CompilerParams(vmem_limit_bytes=mib << 20, **kw)


def all_to_all(value):
    return lax.all_to_all(value, AXES, split_axis=0, concat_axis=0, tiled=True)


def mate(value):
    count = lax.axis_size("ctx")
    return lax.ppermute(value, "ctx", [(i, i ^ 1) for i in range(count)])


def swap_inner(value):
    heads = lax.axis_size("heads")
    return lax.ppermute(value, "heads", [(h, h ^ 1) for h in range(heads)])


def swap_outer(value):
    heads, ctx = lax.axis_size("heads"), lax.axis_size("ctx")
    pairs = []
    for i in range(1, heads * ctx - 1):
        j = i + 1 if i % 2 else i - 1
        pairs.append(tuple(b % heads * ctx + b // heads for b in (i, j)))
    return lax.ppermute(value, ("heads", "ctx"), pairs)


def fetch_outer(own, inner):
    heads, ctx = lax.axis_size("heads"), lax.axis_size("ctx")
    count = heads * ctx
    pairs = []
    for i in range(count):
        step = 1 if i % 2 else -1
        j = i - 2 * step if i // heads % MATES else i + step
        if 0 <= j < count:
            pairs.append(tuple(b % heads * ctx + b // heads for b in (i, j)))
    value = jnp.where(lax.axis_index("ctx") % MATES == 0, own, inner)
    return lax.ppermute(value, ("heads", "ctx"), pairs)


def pack_kernel(k_ref, v_ref, out_ref):
    for g in range(KVH):
        cols = slice(g * HD, (g + 1) * HD)
        out_ref[0, g] = k_ref[:, cols]
        out_ref[1, g] = v_ref[:, cols]


def pack(keys, values):
    return pl.pallas_call(
        pack_kernel,
        out_shape=jax.ShapeDtypeStruct((2, KVH, BLK, HD), BF16),
        compiler_params=params(58),
        name="pack",
    )(keys, values)


def side_of(i, heads):
    return i // heads % MATES


def select_kernel(heads, wanted_ref, in_ref, out_ref):
    count = in_ref.shape[0]
    globs = [in_ref[wanted_ref[count + slot]] for slot in range(NG)]
    for i in range(count):
        out_ref[i, 0] = in_ref[wanted_ref[i]]
        out_ref[i, 1] = globs[side_of(i, heads)]


def select(wanted, slices, heads):
    count, rows, _ = slices.shape
    if rows % 16:
        i = jnp.arange(count)
        glob = wanted[count + side_of(i, heads)]
        return slices[jnp.stack([wanted[i], glob], axis=1)]
    return pl.pallas_call(
        lambda *refs: select_kernel(heads, *refs),
        out_shape=jax.ShapeDtypeStruct((count, 2, rows, HD), BF16),
        in_specs=[
            pl.BlockSpec(memory_space=pltpu.SMEM),
            pl.BlockSpec(memory_space=pltpu.VMEM),
        ],
        out_specs=pl.BlockSpec(memory_space=pltpu.VMEM),
        compiler_params=params(8),
        name="select",
    )(wanted, slices)


def combine_kernel(heads, wanted_ref, in_ref, out_ref, acc_ref):
    count = in_ref.shape[0]
    acc_ref[...] = jnp.zeros_like(acc_ref)
    for side in range(MATES):
        total = None
        for i in range(count):
            if side_of(i, heads) == side:
                term = in_ref[i, 1].astype(F32)
                total = term if total is None else total + term
        acc_ref[wanted_ref[count + side]] += total
    for i in range(count):
        acc_ref[wanted_ref[i]] += in_ref[i, 0].astype(F32)
    out_ref[...] = acc_ref[...].astype(BF16)


def combine(wanted, terms, heads):
    count, _, rows, _ = terms.shape
    if rows % 16:
        i = jnp.arange(count)
        wide = terms.astype(F32)
        total = jnp.zeros((count, rows, HD), F32).at[wanted[i]].add(wide[:, 0])
        return total.at[wanted[count + side_of(i, heads)]].add(wide[:, 1]).astype(BF16)
    return pl.pallas_call(
        lambda *refs: combine_kernel(heads, *refs),
        out_shape=jax.ShapeDtypeStruct((count, rows, HD), BF16),
        in_specs=[
            pl.BlockSpec(memory_space=pltpu.SMEM),
            pl.BlockSpec(memory_space=pltpu.VMEM),
        ],
        out_specs=pl.BlockSpec(memory_space=pltpu.VMEM),
        scratch_shapes=[pltpu.VMEM((count, rows, HD), F32)],
        compiler_params=params(16),
        name="combine",
    )(wanted, terms)


def join_kernel(random_ref, glob_ref, other_ref, out_ref):
    out_ref[:, 0] = random_ref[...]
    out_ref[:, 1] = (glob_ref[...] + other_ref[...].astype(F32)).astype(BF16)


def join(random, glob, other):
    count, rows, _ = random.shape
    if rows % 16:
        total = (glob + other.astype(F32)).astype(BF16)
        return jnp.stack([random, total], axis=1)
    return pl.pallas_call(
        join_kernel,
        out_shape=jax.ShapeDtypeStruct((count, 2, rows, HD), BF16),
        compiler_params=params(8),
        name="join",
    )(random, glob, other)


def stacked(ref):
    return jnp.concatenate(
        [ref[:, h * HD : (h + 1) * HD] for h in range(GROUP)], axis=0
    )


def blocks_of(near, far_ref, other_ref):
    blocks = list(near)
    for ref, slot in ((far_ref, 1), (other_ref, 1), (far_ref, 0)):
        blocks.append(ref[:, slot].reshape(BLK, HD))
    return blocks


def dot_nt(a, b):
    return lax.dot_general(a, b, NT, preferred_element_type=F32)


def put_grads(rows, queries, douts, probs_ref, ds_ref, dests):
    dk = jnp.dot(ds_ref[rows], queries, preferred_element_type=F32) * SCALE
    dv = jnp.dot(probs_ref[rows], douts, preferred_element_type=F32)
    for i, dest in enumerate(dests):
        for kind, term in enumerate((dk, dv)):
            dest[kind] = term[i * BLK : (i + 1) * BLK].astype(dest.dtype)


def block_rows(b):
    return slice(b * BLK, (b + 1) * BLK)


def masked(edge_ref, b, scores):
    return jnp.where(edge_ref[0] == 0, scores, NEG_FILL) if b == 1 else scores


def first_kernel(q_ref, do_ref, own_ref, inner_ref, stats_ref):
    keys, values = (
        jnp.concatenate([own_ref[kind, 0], inner_ref[kind, 0]], axis=0)
        for kind in range(2)
    )
    queries, douts = stacked(q_ref), stacked(do_ref)
    for part in range(WIDE // PART):
        cols = slice(part * PART, (part + 1) * PART)
        s, dp = dot_nt(keys, queries[cols]), dot_nt(values, douts[cols])
        row_max = jnp.max(s, axis=0, keepdims=True)
        w = jnp.exp2((s - row_max) * FACTOR)
        stats_ref[0, 0:1, cols] = row_max
        stats_ref[0, 1:2, cols] = jnp.sum(w, axis=0, keepdims=True)
        stats_ref[0, 2:3, cols] = jnp.sum(w * dp, axis=0, keepdims=True)


def scores_kernel(
    edge_ref, far_ref, other_ref, first_ref, q_any, do_any, outer_any,
    stats_ref, glob_ref, mate_ref, random_ref,
    s_ref, dp_ref, probs_ref, ds_ref, outer_ref, tokens_ref, sem, token_sem,
):
    outer_copy = pltpu.make_async_copy(outer_any, outer_ref, sem)

    def token_copies(g):
        cols = pl.ds(pl.multiple_of(g * WIDE, WIDE), WIDE)
        return [
            pltpu.make_async_copy(
                ref.at[:, cols], tokens_ref.at[i, g], token_sem.at[i, g]
            )
            for i, ref in enumerate((q_any, do_any))
        ]

    outer_copy.start()
    for g in range(KVH):
        for copy in token_copies(g):
            copy.start()
    outer_copy.wait()
    share = far_ref.shape[1] // KVH
    count = SLOTS - 2

    def group(g, carry):
        for copy in token_copies(g):
            copy.wait()
        queries, douts = (stacked(tokens_ref.at[i, g]) for i in range(2))
        keys, values = (
            blocks_of(
                [outer_ref[kind, g]],
                far_ref.at[kind, pl.ds(g * share, share)],
                other_ref.at[kind, pl.ds(g * share, share)],
            )
            for kind in range(2)
        )
        for piece in range(WIDE // PIECE):
            cols = slice(piece * PIECE, (piece + 1) * PIECE)
            first_max = first_ref[g, 0:1, cols]
            row_max = first_max
            for b in range(count):
                score = dot_nt(keys[b], queries[cols])
                if b == 0:
                    score = jnp.where(edge_ref[0] == 0, score, NEG_FILL)
                s_ref[block_rows(b)] = score
                row_max = jnp.maximum(row_max, jnp.max(score, axis=0, keepdims=True))
            scale = jnp.exp2((first_max - row_max) * FACTOR)
            row_sum = first_ref[g, 1:2, cols] * scale
            centre = first_ref[g, 2:3, cols] * scale
            for b in range(count):
                w = jnp.exp2((s_ref[block_rows(b)] - row_max) * FACTOR)
                if b >= 1:
                    s_ref[block_rows(b)] = w
                dp = dot_nt(values[b], douts[cols])
                dp_ref[block_rows(b)] = dp
                row_sum = row_sum + jnp.sum(w, axis=0, keepdims=True)
                centre = centre + jnp.sum(w * dp, axis=0, keepdims=True)
            inverse = 1.0 / row_sum
            centre = centre * inverse
            stats_ref[g, 0:1, cols] = row_max
            stats_ref[g, 1:2, cols] = inverse
            stats_ref[g, 2:3, cols] = centre
            for b in range(1, count):
                rows = block_rows(b)
                p = s_ref[rows] * inverse
                dest = block_rows(b - 1)
                probs_ref[dest, cols] = p.astype(BF16)
                ds_ref[dest, cols] = (p * (dp_ref[rows] - centre)).astype(BF16)
        dests = [ref.at[:, g] for ref in (glob_ref, mate_ref, random_ref)]
        put_grads(slice(None), queries, douts, probs_ref, ds_ref, dests)
        return carry

    lax.fori_loop(0, KVH, group, 0)


def again(edge_ref, first, keys, values, q, do, stats_ref, probs_ref, ds_ref, cols):
    row_max, inverse, centre = (stats_ref[0, i : i + 1, cols] for i in range(3))
    s, dp = dot_nt(keys, q), dot_nt(values, do)
    for b in range(keys.shape[0] // BLK):
        rows = block_rows(b)
        score = masked(edge_ref, first + b, s[rows])
        p = jnp.exp2((score - row_max) * FACTOR) * inverse
        probs_ref[rows, cols] = p.astype(BF16)
        ds_ref[rows, cols] = (p * (dp[rows] - centre)).astype(BF16)


def window_kernel(
    edge_ref, q_ref, do_ref, inner_ref, outer_ref, stats_ref,
    to_inner_ref, to_outer_ref, probs_ref, ds_ref,
):
    keys, values = (
        jnp.concatenate([inner_ref[kind, 0], outer_ref[kind, 0]], axis=0)
        for kind in range(2)
    )
    queries, douts = stacked(q_ref), stacked(do_ref)
    for part in range(WIDE // PART):
        cols = slice(part * PART, (part + 1) * PART)
        again(
            edge_ref, 0, keys, values, queries[cols], douts[cols],
            stats_ref, probs_ref, ds_ref, cols,
        )
    put_grads(
        slice(None), queries, douts, probs_ref, ds_ref,
        (to_inner_ref.at[:, 0], to_outer_ref.at[:, 0]),
    )


def outputs_kernel(
    edge_ref, q_ref, do_ref, own_ref, inner_ref, outer_ref, far_ref, other_ref,
    stats_ref, from_inner_ref, from_outer_ref, out_ref, dq_ref, near_ref, probs_ref, ds_ref,
):
    key_blocks, value_blocks = (
        blocks_of(
            [ref[kind, 0] for ref in (inner_ref, outer_ref, own_ref)],
            far_ref.at[kind],
            other_ref.at[kind],
        )
        for kind in range(2)
    )
    keys, values = (jnp.concatenate(x, axis=0) for x in (key_blocks, value_blocks))
    keys_t, values_t = (
        jnp.concatenate([x.T for x in blocks], axis=1)
        for blocks in (key_blocks, value_blocks)
    )
    queries, douts = stacked(q_ref), stacked(do_ref)
    for part in range(WIDE // PART):
        cols = slice(part * PART, (part + 1) * PART)
        again(
            edge_ref, 0, keys, values, queries[cols], douts[cols],
            stats_ref, probs_ref, ds_ref, cols,
        )
        out_t = jnp.dot(values_t, probs_ref[:, cols], preferred_element_type=F32)
        dq_t = jnp.dot(keys_t, ds_ref[:, cols], preferred_element_type=F32) * SCALE
        for i in range(PART // HD):
            place = slice(i * HD, (i + 1) * HD)
            dest = slice(part * PART + i * HD, part * PART + (i + 1) * HD)
            out_ref[:, dest] = out_t[:, place].T.astype(BF16)
            dq_ref[:, dest] = dq_t[:, place].T.astype(BF16)
    put_grads(block_rows(2), queries, douts, probs_ref, ds_ref, (near_ref.at[:, 0],))
    for kind in range(2):
        back = from_inner_ref[kind, 0].astype(F32) + from_outer_ref[kind, 0].astype(F32)
        near_ref[kind, 0] += back


def finish_kernel(near_ref, far_ref, dk_ref, dv_ref):
    for kind, dest in enumerate((dk_ref, dv_ref)):
        for g in range(KVH):
            total = near_ref[kind, g] + far_ref[kind, g].astype(F32)
            dest[:, g * HD : (g + 1) * HD] = total.astype(BF16)


def finish(near, far):
    shape = jax.ShapeDtypeStruct((BLK, KVH * HD), BF16)
    return pl.pallas_call(
        finish_kernel,
        out_shape=(shape, shape),
        compiler_params=params(8),
        name="finish",
    )(near, far)


def shards(queries, keys_in, values_in, cotangent, rand_blocks, glob_blocks):
    heads, ctx = lax.axis_size("heads"), lax.axis_size("ctx")
    count = heads * ctx
    mine = lax.axis_index("ctx") * heads + lax.axis_index("heads")
    edges = ((mine == 0) | (mine == count - 1)).astype(jnp.int32).reshape(1)
    wanted = jnp.concatenate([rand_blocks[:, 0], glob_blocks])
    rows = 2 * KVH * BLK // count
    share = BLK // rows if rows % 16 == 0 else 1
    token = pl.BlockSpec((BLK, WIDE), lambda g: (0, g))
    block = pl.BlockSpec((2, 1, BLK, HD), lambda g: (0, g, 0, 0))
    far_spec = pl.BlockSpec((2, share, 2, BLK // share, HD), lambda g: (0, g, 0, 0, 0))
    stat = pl.BlockSpec((1, 8, WIDE), lambda g: (g, 0, 0))
    vmem = pl.BlockSpec(memory_space=pltpu.VMEM)
    smem = pl.BlockSpec(memory_space=pltpu.SMEM)
    anywhere = pl.BlockSpec(memory_space=pl.ANY)
    low, wide = (jax.ShapeDtypeStruct((2, KVH, BLK, HD), dtype) for dtype in (BF16, F32))
    stat_shape = jax.ShapeDtypeStruct((KVH, 8, WIDE), F32)
    token_shape = jax.ShapeDtypeStruct(queries.shape, BF16)
    flops = 2 * H * BLK * SLOTS * BLK * HD

    def call(kernel, name, work, mib, ins, outs, scratch=(), **kw):
        return pl.pallas_call(
            kernel,
            in_specs=ins,
            out_specs=[spec for spec, _ in outs],
            out_shape=[shape for _, shape in outs],
            scratch_shapes=scratch,
            compiler_params=params(mib),
            cost_estimate=pl.CostEstimate(
                flops=int(work * flops), bytes_accessed=4 << 20, transcendentals=0
            ),
            name=name,
            **kw,
        )

    def low_pair(length):
        return [pltpu.VMEM((length * BLK, WIDE), BF16)] * 2

    grid = (KVH,)
    packed = pack(keys_in, values_in)
    slices = all_to_all(packed.reshape(count, rows, HD))
    inner = swap_inner(packed)
    slices, inner = lax.optimization_barrier((slices, inner))
    outer = fetch_outer(packed, inner)
    far = all_to_all(select(wanted, slices, heads))
    first = call(
        first_kernel, "first", 1, 53, [token, token, block, block],
        [(stat, stat_shape)], grid=grid,
    )(queries, cotangent, packed, inner)[0]
    far, outer, first = lax.optimization_barrier((far, outer, first))
    if share == 1:
        far = far.reshape(2, KVH, BLK // rows, 2, rows, HD)
        far = jnp.transpose(far, (0, 1, 3, 2, 4, 5))
    far = far.reshape(2, KVH * share, 2, BLK // share, HD)
    other = mate(far)
    stats, glob, for_mate, random = call(
        scores_kernel,
        "scores",
        3,
        50,
        [smem, vmem, vmem, vmem] + [anywhere] * 3,
        [(vmem, stat_shape), (vmem, wide)] + [(vmem, low)] * 2,
        [pltpu.VMEM(((SLOTS - 2) * BLK, PIECE), F32)] * 2
        + low_pair(3)
        + [
            pltpu.VMEM((2, KVH, BLK, HD), BF16),
            pltpu.VMEM((2, KVH, BLK, WIDE), BF16),
            pltpu.SemaphoreType.DMA,
            pltpu.SemaphoreType.DMA((2, KVH)),
        ],
    )(edges, far, other, first, queries, cotangent, outer)
    flat = (count, rows, HD)
    terms = join(random.reshape(flat), glob.reshape(flat), mate(for_mate).reshape(flat))
    arrived = all_to_all(terms)
    back = call(
        window_kernel, "window", 1, 53, [smem, token, token, block, block, stat],
        [(block, low)] * 2, low_pair(2), grid=grid,
    )(edges, queries, cotangent, inner, outer, stats)
    back = [swap_inner(back[0]), swap_outer(back[1])]
    arrived, *back = lax.optimization_barrier((arrived, *back))
    summed = combine(wanted, arrived, heads)
    returned = all_to_all(summed).reshape(2, KVH, BLK, HD)
    stats, summed = lax.optimization_barrier((stats, summed))
    attn_out, grad_query, near = call(
        outputs_kernel,
        "outputs",
        3,
        52,
        [smem, token, token] + [block] * 3 + [far_spec] * 2 + [stat, block, block],
        [(token, token_shape)] * 2 + [(block, wide)],
        low_pair(SLOTS),
        grid=grid,
    )(edges, queries, cotangent, packed, inner, outer, far, other, stats, *back)
    grad_keys, grad_values = finish(near, returned)
    return attn_out, grad_query, grad_keys, grad_values


def solution(mesh):
    spec = P(AXES, None)
    return jax.shard_map(
        shards,
        mesh=mesh,
        in_specs=(spec, spec, spec, spec, P(), P()),
        out_specs=(spec, spec, spec, spec),
        check_vma=False,
    )
```
